128 devices in a mesh: leaf: 64 (over z, y, x_hi, core), blk: 2 (over x_lo).
Axes of the slice: x: 4 (x_hi: 2, x_lo: 2; x = x_hi * 2 + x_lo), y: 4, z: 4, core: 2. Of those that a mesh axis runs over, the one named last changes fastest.
Arguments:
- schur_leaf: bfloat16 [128, 1024, 1024], P(('leaf', 'blk')), may hold values from -0.59765625 to 0.59765625
- tiles_one: bfloat16 [128, 16, 128, 128], P(('leaf', 'blk')), may hold values from -0.59765625 to 0.59765625
- rows_one: int32 [128, 16], P(('leaf', 'blk')), may hold values from 0 to 7
- cols_one: int32 [128, 16], P(('leaf', 'blk')), may hold values from 0 to 7
- count_one: int32 [128], P(('leaf', 'blk')), may hold values from 5 to 16, as said below
- order_one: int32 [64, 16, 128], replicated, may hold values from 0 to 127, each once within a row
- inverse_one: float32 [128, 8, 64, 64], P(('leaf', 'blk')), may hold values from -0.75 to 0.75
- tiles_two: bfloat16 [128, 16, 128, 128], P(('leaf', 'blk')), may hold values from -1.796875 to 1.796875
- rows_two: int32 [128, 16], P(('leaf', 'blk')), may hold values from 0 to 7
- cols_two: int32 [128, 16], P(('leaf', 'blk')), may hold values from 0 to 3
- count_two: int32 [128], P(('leaf', 'blk')), may hold values from 5 to 16, as said below
- order_two: int32 [32, 16, 128], replicated, may hold values from 0 to 127, each once within a row
- inverse_two: float32 [128, 4, 64, 64], P(('leaf', 'blk')), may hold values from -0.075 to 0.075
Outputs:
- schur_top: bfloat16 [128, 1024, 256], P(('leaf', 'blk'))
The draws below stay inside these ranges and needn't reach their ends.
Inputs may be any that keep to these rules, and one draw needn't show every extreme that they name: `count_one`: some box has all 16 slots live and some only 5. `count_two`: some box has all 16 slots live and some only 5.
All inputs are finite; a program needn't handle non-finite values.
Results may differ from the reference program's by a relative error of at most 0.0056.
Values may be sent and summed in bfloat16 or wider, within the bound.
A program may use at most 64 MiB of HBM per device.

```python
import jax
import jax.numpy as jnp
from jax import lax

W = 1024
BLOCK = 128
NT = 16
BOXES = 128


def draw_counts(key):
    total = BOXES
    values = jax.random.randint(key, (total,), NT // 3, NT + 1)
    where_high = jax.random.randint(jax.random.fold_in(key, 1), (), 0, total)
    shift_by = jax.random.randint(jax.random.fold_in(key, 2), (), 1, total)
    values = values.at[where_high].set(NT)
    values = values.at[(where_high + shift_by) % total].set(NT // 3)
    return values.astype(jnp.int32)


def draw_count_one(key, part):
    return draw_counts(jax.random.fold_in(key, 11))


def draw_count_two(key, part):
    return draw_counts(jax.random.fold_in(key, 12))


def set_ends(entries, own_key, least, largest):
    longest = entries.shape.index(max(entries.shape))
    spots = []
    for shift in (0, 1):
        where = [jax.random.randint(jax.random.fold_in(own_key, axis), (), 0, length) for axis, length in enumerate(entries.shape)]
        where[longest] = (where[longest] + shift) % entries.shape[longest]
        spots.append(tuple(where))
    return entries.at[spots[0]].set(least).at[spots[1]].set(largest)


def level_of(stream_key, extent, pieces, smallest, top_value):
    factor_of, own = 1.0, jax.random.fold_in(stream_key, 6)
    for axis_at, parts in pieces:
        heights = jnp.exp(jax.random.uniform(jax.random.fold_in(own, axis_at), (parts,), jnp.float32, smallest / len(pieces), top_value / len(pieces)))
        factor_of = factor_of * jnp.repeat(heights, extent[axis_at] // parts).reshape([-1 if axis == axis_at else 1 for axis in range(len(extent))])
    return factor_of


def centred(key, shape, scale, bound, shards=(), kind=jnp.bfloat16):
    values = scale * jax.random.normal(key, shape, jnp.float32)
    if shards:
        values = values * level_of(key, shape, shards, -0.22, 0.18)
    return jnp.clip(values, -bound, bound).astype(kind)


def setup_inputs(seed: int = 0) -> dict:
    arg_keys = jax.random.split(jax.random.key(seed), 14)
    return {
        "schur_leaf": centred(arg_keys[0], (BOXES, W, W), 0.1, 0.59765625, ((0, 128),)),
        "tiles_one": centred(arg_keys[1], (BOXES, NT, BLOCK, BLOCK), 0.1, 0.59765625, ((0, 128),)),
        "rows_one": set_ends(jax.random.randint(arg_keys[2], (BOXES, NT), 0, W // BLOCK), jax.random.fold_in(arg_keys[2], 1), 0, (W // BLOCK) - 1).astype(jnp.int32),
        "cols_one": set_ends(jax.random.randint(arg_keys[3], (BOXES, NT), 0, W // BLOCK), jax.random.fold_in(arg_keys[3], 1), 0, (W // BLOCK) - 1).astype(jnp.int32),
        "count_one": draw_count_one(jax.random.fold_in(arg_keys[13], 71), 0),
        "order_one": jax.vmap(lambda own: jax.random.permutation(own, BLOCK))(jax.random.split(arg_keys[5], (BOXES // 2) * (2 * W // BLOCK))).reshape((BOXES // 2, 2 * W // BLOCK, BLOCK)).astype(jnp.int32),
        "inverse_one": centred(arg_keys[6], (BOXES, W // BLOCK, BLOCK // 2, BLOCK // 2), 0.125, 0.75, ((0, 128),), jnp.float32),
        "tiles_two": centred(arg_keys[7], (BOXES, NT, BLOCK, BLOCK), 0.3, 1.796875, ((0, 128),)),
        "rows_two": set_ends(jax.random.randint(arg_keys[8], (BOXES, NT), 0, W // BLOCK), jax.random.fold_in(arg_keys[8], 1), 0, (W // BLOCK) - 1).astype(jnp.int32),
        "cols_two": set_ends(jax.random.randint(arg_keys[9], (BOXES, NT), 0, W // (2 * BLOCK)), jax.random.fold_in(arg_keys[9], 1), 0, (W // (2 * BLOCK)) - 1).astype(jnp.int32),
        "count_two": draw_count_two(jax.random.fold_in(arg_keys[13], 71), 0),
        "order_two": jax.vmap(lambda own: jax.random.permutation(own, BLOCK))(jax.random.split(arg_keys[11], (BOXES // 4) * (2 * W // BLOCK))).reshape((BOXES // 4, 2 * W // BLOCK, BLOCK)).astype(jnp.int32),
        "inverse_two": centred(arg_keys[12], (BOXES, W // (2 * BLOCK), BLOCK // 2, BLOCK // 2), 0.0125, 0.075, ((0, 128),), jnp.float32),
    }


def pick_one(array, index):
    return lax.dynamic_index_in_dim(array, index, 0, keepdims=False)


def couple_tiles(tile_set, row_block, col_block, live_mask, row_blocks, col_blocks, block_size):
    count_tiles = tile_set.shape[0]
    target = row_block * col_blocks + col_block
    onehot = ((jnp.arange(row_blocks * col_blocks, dtype=jnp.int32)[:, None] == target[None, :]) & live_mask[None, :]).astype(jnp.bfloat16)
    blocks = jnp.dot(onehot, tile_set.reshape(count_tiles, block_size * block_size), preferred_element_type=jnp.float32)
    return blocks.reshape(row_blocks, col_blocks, block_size, block_size).transpose(0, 2, 1, 3).reshape(row_blocks * block_size, col_blocks * block_size)


def eliminate_whole(merged, order_set, inverses):
    block_total = order_set.shape[0]
    block_size = order_set.shape[1]
    keep_size = block_size // 2
    starts = jnp.arange(block_total, dtype=jnp.int32)[:, None] * block_size
    skel_rows = (starts + order_set[:, :keep_size]).reshape(-1)
    redundant = (starts + order_set[:, keep_size:]).reshape(-1)
    upper_rows = jnp.take(merged, skel_rows, axis=0)
    kept_part = jnp.take(upper_rows, skel_rows, axis=1)
    coupled = jnp.take(upper_rows, redundant, axis=1).reshape(-1, block_total, keep_size)
    weighted = jnp.einsum("rbt,btu->rbu", coupled, inverses, precision=lax.Precision.HIGHEST)
    weighted = weighted.reshape(coupled.shape[0], -1).astype(jnp.bfloat16)
    lower_rows = jnp.take(jnp.take(merged, redundant, axis=0), skel_rows, axis=1).astype(jnp.bfloat16)
    return kept_part - jnp.dot(weighted, lower_rows, preferred_element_type=jnp.float32)


def reference(schur_leaf, tiles_one, rows_one, cols_one, count_one, order_one, inverse_one, tiles_two, rows_two, cols_two, count_two, order_two, inverse_two):
    blocks = W // BLOCK
    slots = jnp.arange(NT, dtype=jnp.int32)[None, :]
    live_one = slots < count_one[:, None]
    live_two = slots < count_two[:, None]

    def first_level(parent):
        upper_box = 4 * (parent // 2) + parent % 2
        lower_box = upper_box + 2
        upper_right = couple_tiles(pick_one(tiles_one, upper_box), pick_one(rows_one, upper_box), pick_one(cols_one, upper_box), pick_one(live_one, upper_box), blocks, blocks, BLOCK)
        lower_left = couple_tiles(pick_one(tiles_one, lower_box), pick_one(rows_one, lower_box), pick_one(cols_one, lower_box), pick_one(live_one, lower_box), blocks, blocks, BLOCK)
        top_left = pick_one(schur_leaf, upper_box).astype(jnp.float32)
        bottom_right = pick_one(schur_leaf, lower_box).astype(jnp.float32)
        merged = jnp.concatenate([jnp.concatenate([top_left, upper_right], 1), jnp.concatenate([lower_left, bottom_right], 1)], 0)
        inverses = jnp.concatenate([pick_one(inverse_one, upper_box), pick_one(inverse_one, lower_box)], 0)
        return eliminate_whole(merged, pick_one(order_one, parent), inverses)

    level_one = lax.map(first_level, jnp.arange(BOXES // 2, dtype=jnp.int32))

    def tiles_of(first_box):
        other_box = first_box + 2
        tile_set = jnp.concatenate([pick_one(tiles_two, first_box), pick_one(tiles_two, other_box)], 0)
        row_block = jnp.concatenate([pick_one(rows_two, first_box), pick_one(rows_two, other_box)], 0)
        col_block = jnp.concatenate([pick_one(cols_two, first_box), pick_one(cols_two, other_box) + blocks // 2], 0)
        live_mask = jnp.concatenate([pick_one(live_two, first_box), pick_one(live_two, other_box)], 0)
        return couple_tiles(tile_set, row_block, col_block, live_mask, blocks, blocks, BLOCK)

    def second_level(parent):
        first_box = 4 * parent
        upper_right = tiles_of(first_box)
        lower_left = tiles_of(first_box + 1)
        merged = jnp.concatenate([jnp.concatenate([pick_one(level_one, 2 * parent), upper_right], 1), jnp.concatenate([lower_left, pick_one(level_one, 2 * parent + 1)], 1)], 0)
        inverses = jnp.concatenate([pick_one(inverse_two, first_box), pick_one(inverse_two, first_box + 2), pick_one(inverse_two, first_box + 1), pick_one(inverse_two, first_box + 3)], 0)
        return eliminate_whole(merged, pick_one(order_two, parent), inverses)

    level_two = lax.map(second_level, jnp.arange(BOXES // 4, dtype=jnp.int32))
    arranged = level_two.reshape(BOXES // 4, W, 2, 2, W // 4).transpose(0, 3, 2, 1, 4).reshape(BOXES, W, W // 4)
    return arranged.astype(jnp.bfloat16)
```

```python
import jax
import jax.numpy as jnp
from jax import lax
from jax.experimental import pallas as pl
from jax.experimental.pallas import tpu as pltpu
from jax.sharding import PartitionSpec as P

MESH = pl.DeviceIdType.MESH
F32 = jnp.float32
BF16 = jnp.bfloat16
NT = 16


def dot(a, b):
    return jnp.dot(a, b, preferred_element_type=F32)


def chain_table(rows, cols, count, width, lane):
    live = count[0]
    targets = [rows[0, n] * width + cols[0, n] for n in range(NT)]
    prev = jnp.zeros((1, 128), jnp.int32)
    last = jnp.zeros((1, 128), jnp.int32)
    for n in range(NT):
        before = jnp.int32(0)
        for m in range(n):
            before = jnp.where((targets[m] == targets[n]) & (m < live), m + 1, before)
        prev = jnp.where(lane == n, before, prev)
        last = jnp.where((lane == targets[n]) & (n < live), n + 1, last)
    return prev, last


def halves(value):
    high = value.astype(BF16)
    return high, (value - high.astype(F32)).astype(BF16)


def kernel(
    a_hbm, t1_hbm, t2_hbm, i1_hbm, i2_hbm, o1_hbm, o2_hbm,
    rows1_hbm, cols1_hbm, count1_hbm, rows2_hbm, cols2_hbm, count2_hbm,
    out_ref,
    rows1, cols1, count1, rows2, cols2, count2,
    a_v, c_v, t1_in, t2_v, i1_v, i2_v, o1_v, o2_v,
    tab, tab_k, tab_x, own_s, k_s, x_s,
    xk, xt, cc, p2r, p2x, g_v, e1_v, e2hi, e2lo, fxhi, fxlo, pack2, pack_x,
    acc1, acco, accx, xq, xq_in,
    ms, mr1, ks, mrc, w1, w1_in,
    lss, lrs, w00, w00_in, w01, w01_in, w10, w10_in,
    bss, brs, bsr, crs, csr, p_out, p_in,
    loc, ksend, krecv, xsend, xrecv,
):
    leaf = lax.axis_index("leaf")
    c = lax.axis_index("blk")
    r = leaf // 2
    h = leaf - 2 * r
    other = 1 - h
    kid = {"leaf": leaf + 1 - 2 * h}
    xid = {"blk": 1 - c}

    def to_k(src, dst, n):
        return pltpu.make_async_remote_copy(
            src_ref=src, dst_ref=dst, send_sem=ksend.at[n], recv_sem=krecv.at[n],
            device_id=kid, device_id_type=MESH,
        )

    def to_x(src, dst, n):
        return pltpu.make_async_remote_copy(
            src_ref=src, dst_ref=dst, send_sem=xsend.at[n], recv_sem=xrecv.at[n],
            device_id=xid, device_id_type=MESH,
        )

    load_o1 = pltpu.make_async_copy(o1_hbm.at[2 * r + c], o1_v, loc.at[0])
    load_o2 = pltpu.make_async_copy(o2_hbm.at[r], o2_v, loc.at[1])
    load_t2 = pltpu.make_async_copy(t2_hbm.at[0], t2_v, loc.at[2])
    load_i2 = pltpu.make_async_copy(i2_hbm.at[0], i2_v, loc.at[3])
    load_i1 = pltpu.make_async_copy(i1_hbm.at[0], i1_v, loc.at[4])
    load_a = pltpu.make_async_copy(a_hbm.at[0], a_v, loc.at[5])
    pairs = (
        (rows1_hbm, rows1), (cols1_hbm, cols1), (count1_hbm, count1),
        (rows2_hbm, rows2), (cols2_hbm, cols2), (count2_hbm, count2),
    )
    load_labels = [pltpu.make_async_copy(src, dst, loc.at[9 + n]) for n, (src, dst) in enumerate(pairs)]
    for load in (*load_labels, load_o1, load_o2, load_t2, load_i2, load_i1, load_a):
        load.start()

    barrier = pltpu.get_barrier_semaphore()
    pl.semaphore_signal(barrier, inc=1, device_id=kid, device_id_type=MESH)
    pl.semaphore_signal(barrier, inc=1, device_id=xid, device_id_type=MESH)
    pl.semaphore_wait(barrier, 2)

    send_t1 = to_k(t1_hbm.at[0], t1_in, 0)
    send_t1.start()

    for load in load_labels:
        load.wait()
    lane = lax.broadcasted_iota(jnp.int32, (1, 128), 1)
    prev1, last1 = chain_table(rows1, cols1, count1, 8, lane)
    prev2, last2 = chain_table(rows2, cols2, count2, 4, lane)
    tab[0:1, :] = prev1
    tab[1:2, :] = last1
    tab[2:3, :] = prev2
    tab[3:4, :] = last2
    tab[4:8, :] = jnp.zeros((4, 128), jnp.int32)
    send_tab_k = to_k(tab, tab_k, 1)
    send_tab_k.start()
    send_tab_x = to_x(tab, tab_x, 0)
    send_tab_x.start()
    own_tab = pltpu.make_async_copy(tab, own_s, loc.at[6])
    own_tab.start()

    load_o1.wait()
    load_o2.wait()
    lane8 = lax.broadcasted_iota(jnp.int32, (8, 128), 1)
    low8 = lane8 < 64
    even = o1_v[pl.ds(0, 8, stride=2), :]
    odd = o1_v[pl.ds(1, 8, stride=2), :]
    shift = jnp.where(low8, 0, 128)
    skel = jnp.where(low8, even, pltpu.roll(odd, 64, 1)) + shift
    redu = jnp.where(low8, pltpu.roll(even, 64, 1), odd) + shift
    base = pl.multiple_of(c * 8, 8)
    mine2 = o2_v[pl.ds(base, 8), :]
    mine2_swapped = pltpu.roll(mine2, 64, 1)
    theirs2 = o2_v[pl.ds(pl.multiple_of(8 - base, 8), 8), :]
    theirs2 = jnp.where(h == 0, theirs2, pltpu.roll(theirs2, 4, 0))
    theirs2_swapped = pltpu.roll(theirs2, 64, 1)
    tall = lax.broadcasted_iota(jnp.int32, (256, 128), 0)
    square = lax.broadcasted_iota(jnp.int32, (128, 128), 0)
    lane128 = lax.broadcasted_iota(jnp.int32, (128, 128), 1)
    low128 = lane128 < 64

    def onehot(rows, index):
        return jnp.where(rows == index, 1.0, 0.0)

    for k in range(8):
        p2r[k] = onehot(square, mine2[k : k + 1, :]).T.astype(BF16)
    for j in range(4):
        index = (theirs2_swapped if j % 2 else theirs2)[j : j + 1, :]
        p2x[j] = onehot(square, index).astype(BF16)

    load_i2.wait()
    for q in range(2):
        pack2[q] = jnp.concatenate([i2_v[2 * q], i2_v[2 * q + 1]], axis=1)
    send_pack = to_x(pack2, pack_x, 1)
    send_pack.start()
    load_t2.wait()
    own_tab.wait()
    acco[0] = jnp.zeros((128, 128), F32)
    low64 = lax.broadcasted_iota(jnp.int32, (64, 128), 1) < 64
    sends_q = []
    for n in range(NT):
        half = dot(t2_v[n], p2x[cols2[0, n]]).astype(BF16)
        tile = dot(p2r[rows2[0, n]], half)
        is_even = (cols2[0, n] & 1) == 0
        take_bottom = low64 == is_even
        xq[n] = jnp.where(take_bottom, tile[64:, :], tile[:64, :]).astype(BF16)
        acco[n + 1] = tile + acco[own_s[2, n]]
        if n % 8 == 7:
            part = pl.ds(n - 7, 8)
            sends_q.append(to_x(xq.at[part], xq_in.at[part], 2 + n // 8))
            sends_q[-1].start()

    for k in range(8):
        os_k = onehot(tall, skel[k : k + 1, :]).astype(BF16)
        or_k = onehot(tall, redu[k : k + 1, :])
        ct = dot(os_k, onehot(square, mine2[k : k + 1, :]).astype(BF16))
        xk[k] = or_k.astype(BF16)
        xt[k, 0:128, :] = ct.T.astype(BF16)
        xt[k, 128:256, :] = or_k.T.astype(BF16)
        if k % 2:
            cc[k] = dot(os_k, onehot(square, mine2_swapped[k : k + 1, :]).astype(BF16)).astype(BF16)
        else:
            cc[k] = ct.astype(BF16)
    low256 = lax.broadcasted_iota(jnp.int32, (256, 128), 1) < 64
    zero = jnp.zeros((256, 128), BF16)
    first = h * 4
    for q in range(2):
        c0 = cc[first + 2 * q]
        c1 = cc[first + 2 * q + 1]
        g_v[q, 0:256, 0:128] = jnp.where(low256, c0, zero)
        g_v[q, 0:256, 128:256] = jnp.where(low256, zero, c0)
        g_v[q, 256:512, 0:128] = jnp.where(low256, zero, c1)
        g_v[q, 256:512, 128:256] = jnp.where(low256, c1, zero)
    load_i1.wait()
    for i in range(4):
        pack = jnp.concatenate([i1_v[2 * i], i1_v[2 * i + 1]], axis=1)
        diag = jnp.concatenate([jnp.where(low64, pack, 0.0), jnp.where(low64, 0.0, pack)], axis=0)
        high, rest = halves(diag)
        e1_v[i, :, 0:128] = dot(xk[first + i], high).astype(BF16)
        e1_v[i, :, 128:256] = dot(xk[first + i], rest).astype(BF16)

    def expand(pack_ref, hi_ref, lo_ref):
        hi_ref[...] = jnp.zeros((256, 256), BF16)
        lo_ref[...] = jnp.zeros((256, 256), BF16)
        for q in range(2):
            pack = pack_ref[q]
            anti = jnp.concatenate([jnp.where(low64, 0.0, pack), jnp.where(low64, pack, 0.0)], axis=0)
            high, rest = halves(anti)
            hi_ref[128 * q : 128 * q + 128, 128 * q : 128 * q + 128] = high
            lo_ref[128 * q : 128 * q + 128, 128 * q : 128 * q + 128] = rest

    expand(pack2, e2hi, e2lo)

    def select_rows(m_ref, hs):
        for i in range(4):
            block = dot(xt[hs * 4 + i], m_ref[256 * i : 256 * i + 256, :]).astype(BF16)
            ms[0, hs, 64 * i : 64 * i + 64, :] = block[0:64, :]
            ms[1, hs, 64 * i : 64 * i + 64, :] = block[64:128, :]
            mr1[hs, 128 * i : 128 * i + 128, :] = block[128:256, :]

    def select_cols(rho, hs):
        for q in range(2):
            part = dot(ms[rho, hs, :, 512 * q : 512 * q + 512], g_v[q]).astype(BF16)
            ks[rho, hs, :, 128 * q : 128 * q + 128] = part[:, 0:128]
            ks[rho, hs, :, 256 + 128 * q : 384 + 128 * q] = part[:, 128:256]
        for i in range(4):
            both = dot(ms[rho, hs, :, 256 * i : 256 * i + 256], e1_v[i])
            w1[rho, hs, :, 128 * i : 128 * i + 128] = (both[:, 0:128] + both[:, 128:256]).astype(BF16)

    def select_lower(hs):
        for q in range(2):
            part = dot(mr1[hs, :, 512 * q : 512 * q + 512], g_v[q]).astype(BF16)
            mrc[hs, :, 128 * q : 128 * q + 128] = part[:, 0:128]
            mrc[hs, :, 256 + 128 * q : 384 + 128 * q] = part[:, 128:256]

    load_a.wait()
    select_rows(a_v, h)
    select_cols(0, h)
    select_cols(1, h)

    send_t1.wait_recv()
    send_tab_k.wait_recv()
    k_tab = pltpu.make_async_copy(tab_k, k_s, loc.at[7])
    k_tab.start()
    k_tab.wait()
    acc1[0] = jnp.zeros((128, 128), F32)
    for n in range(NT):
        acc1[n + 1] = t1_in[n].astype(F32) + acc1[k_s[0, n]]
    for i in range(8):
        for j in range(8):
            c_v[128 * i : 128 * i + 128, 128 * j : 128 * j + 128] = acc1[k_s[1, 8 * i + j]].astype(BF16)
    select_rows(c_v, other)
    select_cols(0, other)
    send_w1a = to_k(w1.at[0], w1_in.at[0], 2)
    send_w1a.start()
    select_cols(1, other)
    send_w1b = to_k(w1.at[1], w1_in.at[1], 3)
    send_w1b.start()
    select_lower(h)
    select_lower(other)

    for i in range(8):
        for q in range(2):
            e_t = acco[own_s[3, 4 * i + 2 * q]]
            o_t = acco[own_s[3, 4 * i + 2 * q + 1]]
            s_cols = jnp.where(low128, e_t, o_t)
            r_cols = jnp.where(low128, o_t, e_t)
            lanes = slice(128 * q, 128 * q + 128)
            bss[64 * i : 64 * i + 64, lanes] = s_cols[0:64, :]
            brs[64 * i : 64 * i + 64, lanes] = s_cols[64:128, :].astype(BF16)
            bsr[64 * i : 64 * i + 64, lanes] = r_cols[0:64, :].astype(BF16)

    send_w1a.wait_recv()
    for hs in range(2):
        own = dot(w1[0, hs], mrc[h])
        far = dot(w1_in[0, hs], mrc[other])
        level = ks[0, hs].astype(F32) - own - far
        lss[hs] = level[:, 0:256]
        high, rest = halves(level[:, 256:512])
        weighted = dot(high, e2hi[...]) + dot(rest, e2hi[...]) + dot(high, e2lo[...])
        w00[256 * hs : 256 * hs + 256, :] = weighted.astype(BF16)
    send_w00 = to_k(w00, w00_in, 4)
    send_w00.start()

    send_pack.wait_recv()
    expand(pack_x, fxhi, fxlo)
    w01[...] = (dot(bsr[...], fxhi[...]) + dot(bsr[...], fxlo[...])).astype(BF16)
    send_w01 = to_k(w01, w01_in, 5)
    send_w01.start()

    send_w00.wait_recv()
    half_own = pl.ds(pl.multiple_of(h * 256, 256), 256)
    half_far = pl.ds(pl.multiple_of(other * 256, 256), 256)
    b_own = brs[half_own, :]
    b_far = brs[half_far, :]
    sends_p = []
    for m in range(4):
        rows = slice(128 * m, 128 * m + 128)
        p_out[rows, :] = (bss[rows, :] - dot(w00[rows, :], b_own) - dot(w00_in[rows, :], b_far)).astype(BF16)
        part = pl.ds(128 * m, 128)
        sends_p.append(to_x(p_out.at[part], p_in.at[part], 4 + m))
        sends_p[-1].start()

    send_tab_x.wait_recv()
    x_tab = pltpu.make_async_copy(tab_x, x_s, loc.at[8])
    x_tab.start()
    x_tab.wait()
    for send in sends_q:
        send.wait_recv()
    accx[0] = jnp.zeros((64, 128), F32)
    for n in range(NT):
        accx[n + 1] = xq_in[n].astype(F32) + accx[x_s[2, n]]
    for i in range(8):
        for q in range(2):
            e_t = accx[x_s[3, 4 * i + 2 * q]]
            o_t = accx[x_s[3, 4 * i + 2 * q + 1]]
            lanes = slice(128 * q, 128 * q + 128)
            crs[64 * i : 64 * i + 64, lanes] = jnp.where(low64, e_t, o_t).astype(BF16)
            csr[64 * i : 64 * i + 64, lanes] = jnp.where(low64, o_t, e_t).astype(BF16)
    w10[...] = (dot(csr[...], e2hi[...]) + dot(csr[...], e2lo[...])).astype(BF16)
    send_w10 = to_k(w10, w10_in, 6)
    send_w10.start()

    send_w1b.wait_recv()
    for hs in range(2):
        own = dot(w1[1, hs], mrc[h, :, 0:256])
        far = dot(w1_in[1, hs], mrc[other, :, 0:256])
        lrs[256 * hs : 256 * hs + 256, :] = (ks[1, hs, :, 0:256].astype(F32) - own - far).astype(BF16)

    send_w01.wait_recv()
    send_w10.wait_recv()
    l_own = lrs[half_own, :]
    l_far = lrs[half_far, :]
    top = pl.multiple_of(c * 512, 512)
    bottom = pl.multiple_of(512 - c * 512, 512)
    for hs in range(2):
        rows = slice(256 * hs, 256 * hs + 256)
        total = lss[hs] - dot(w00[rows, :], l_own) - dot(w00_in[rows, :], l_far)
        total = total - dot(w01[rows, :], crs[half_own, :]) - dot(w01_in[rows, :], crs[half_far, :])
        out_ref[0, pl.ds(top + 256 * hs, 256), :] = total.astype(BF16)
        total = dot(w10[rows, :], l_own) + dot(w10_in[rows, :], l_far)
        for m in range(2):
            sends_p[2 * hs + m].wait_recv()
        out_ref[0, pl.ds(bottom + 256 * hs, 256), :] = (p_in[rows, :].astype(F32) - total).astype(BF16)

    for send in (send_t1, send_tab_k, send_tab_x, send_pack, *sends_q, send_w1a, send_w1b, send_w00, send_w01, *sends_p, send_w10):
        send.wait_send()


def local(*args):
    schur, t1, rows1, cols1, count1, o1, i1, t2, rows2, cols2, count2, o2, i2 = args
    hbm = pl.BlockSpec(memory_space=pltpu.HBM)
    label = pltpu.SMEM((1, 16), jnp.int32)
    count = pltpu.SMEM((1,), jnp.int32)
    vmem = pltpu.VMEM
    scratch = [
        label, label, count, label, label, count,
        vmem((1024, 1024), BF16), vmem((1024, 1024), BF16), vmem((16, 128, 128), BF16), vmem((16, 128, 128), BF16),
        vmem((8, 64, 64), F32), vmem((4, 64, 64), F32), vmem((16, 128), jnp.int32), vmem((16, 128), jnp.int32),
        vmem((8, 128), jnp.int32), vmem((8, 128), jnp.int32), vmem((8, 128), jnp.int32),
        pltpu.SMEM((8, 128), jnp.int32), pltpu.SMEM((8, 128), jnp.int32), pltpu.SMEM((8, 128), jnp.int32),
        vmem((8, 256, 128), BF16), vmem((8, 256, 256), BF16), vmem((8, 256, 128), BF16), vmem((8, 128, 128), BF16),
        vmem((4, 128, 128), BF16), vmem((2, 512, 256), BF16), vmem((4, 256, 256), BF16),
        vmem((256, 256), BF16), vmem((256, 256), BF16), vmem((256, 256), BF16), vmem((256, 256), BF16),
        vmem((2, 64, 128), F32), vmem((2, 64, 128), F32),
        vmem((17, 128, 128), F32), vmem((17, 128, 128), F32), vmem((17, 64, 128), F32),
        vmem((16, 64, 128), BF16), vmem((16, 64, 128), BF16),
        vmem((2, 2, 256, 1024), BF16), vmem((2, 512, 1024), BF16), vmem((2, 2, 256, 512), BF16), vmem((2, 512, 512), BF16),
        vmem((2, 2, 256, 512), BF16), vmem((2, 2, 256, 512), BF16),
        vmem((2, 256, 256), F32), vmem((512, 256), BF16), vmem((512, 256), BF16), vmem((512, 256), BF16),
        vmem((512, 256), BF16), vmem((512, 256), BF16), vmem((512, 256), BF16), vmem((512, 256), BF16),
        vmem((512, 256), F32), vmem((512, 256), BF16), vmem((512, 256), BF16), vmem((512, 256), BF16),
        vmem((512, 256), BF16), vmem((512, 256), BF16), vmem((512, 256), BF16),
        pltpu.SemaphoreType.DMA((15,)), pltpu.SemaphoreType.DMA((7,)), pltpu.SemaphoreType.DMA((7,)),
        pltpu.SemaphoreType.DMA((8,)), pltpu.SemaphoreType.DMA((8,)),
    ]
    return pl.pallas_call(
        kernel,
        out_shape=jax.ShapeDtypeStruct((1, 1024, 256), BF16),
        in_specs=[hbm] * 13,
        out_specs=pl.BlockSpec(memory_space=pltpu.VMEM),
        scratch_shapes=scratch,
        compiler_params=pltpu.CompilerParams(
            collective_id=0, has_side_effects=True, vmem_limit_bytes=67043328
        ),
    )(schur, t1, t2, i1, i2, o1, o2, rows1, cols1, count1, rows2, cols2, count2)


def solution(mesh):
    boxes = ("leaf", "blk")
    return jax.shard_map(
        local,
        mesh=mesh,
        in_specs=(
            P(boxes, None, None),
            P(boxes, None, None, None),
            P(boxes, None),
            P(boxes, None),
            P(boxes),
            P(),
            P(boxes, None, None, None),
            P(boxes, None, None, None),
            P(boxes, None),
            P(boxes, None),
            P(boxes),
            P(),
            P(boxes, None, None, None),
        ),
        out_specs=P(boxes, None, None),
        check_vma=False,
    )
```

```python
import jax
import jax.numpy as jnp
from jax import lax
from jax.experimental import pallas as pl
from jax.experimental.pallas import tpu as pltpu
from jax.sharding import PartitionSpec as P

MESH = pl.DeviceIdType.MESH
F32 = jnp.float32
BF16 = jnp.bfloat16
NT = 16


def dot(a, b):
    return jnp.dot(a, b, preferred_element_type=F32)


def chain_table(rows, cols, count, width, lane):
    live = count[0]
    targets = [rows[0, n] * width + cols[0, n] for n in range(NT)]
    prev = jnp.zeros((1, 128), jnp.int32)
    last = jnp.zeros((1, 128), jnp.int32)
    for n in range(NT):
        before = jnp.int32(0)
        for m in range(n):
            before = jnp.where((targets[m] == targets[n]) & (m < live), m + 1, before)
        prev = jnp.where(lane == n, before, prev)
        last = jnp.where((lane == targets[n]) & (n < live), n + 1, last)
    return prev, last


def halves(value):
    high = value.astype(BF16)
    return high, (value - high.astype(F32)).astype(BF16)


def kernel(
    a_hbm, t1_hbm, t2_hbm, i1_hbm, i2_hbm, o1_hbm, o2_hbm,
    rows1_hbm, cols1_hbm, count1_hbm, rows2_hbm, cols2_hbm, count2_hbm,
    out_ref,
    rows1, cols1, count1, rows2, cols2, count2,
    a_v, b_v, c_v, t1_v, t1_in, t2_v, i1_v, i2_v, o1_v, o2_v,
    tab, tab_k, tab_x, own_s, k_s, x_s,
    xt, yk, orp, p2l, p2x,
    acca, accb, acco, accx, acca16, accb16, xq, xq_in,
    ms, mu, ks, u1, sr, spart,
    lss, lsr, lsr_in, uu, vown, vx,
    bss, bsr, bsr_in, csr, csr_in, p_out, p_in,
    loc, ksend, krecv, xsend, xrecv,
):
    leaf = lax.axis_index("leaf")
    c = lax.axis_index("blk")
    r = leaf // 2
    h = leaf - 2 * r
    other = 1 - h
    kid = {"leaf": leaf + 1 - 2 * h}
    xid = {"blk": 1 - c}

    def to_k(src, dst, n):
        return pltpu.make_async_remote_copy(
            src_ref=src, dst_ref=dst, send_sem=ksend.at[n], recv_sem=krecv.at[n],
            device_id=kid, device_id_type=MESH,
        )

    def to_x(src, dst, n):
        return pltpu.make_async_remote_copy(
            src_ref=src, dst_ref=dst, send_sem=xsend.at[n], recv_sem=xrecv.at[n],
            device_id=xid, device_id_type=MESH,
        )

    barrier = pltpu.get_barrier_semaphore()
    pl.semaphore_signal(barrier, inc=1, device_id=xid, device_id_type=MESH)
    pl.semaphore_signal(barrier, inc=1, device_id=kid, device_id_type=MESH)

    pairs = (
        (rows1_hbm, rows1), (cols1_hbm, cols1), (count1_hbm, count1),
        (rows2_hbm, rows2), (cols2_hbm, cols2), (count2_hbm, count2),
    )
    load_labels = [pltpu.make_async_copy(src, dst, loc.at[9 + n]) for n, (src, dst) in enumerate(pairs)]
    load_o1 = pltpu.make_async_copy(o1_hbm.at[2 * r + c], o1_v, loc.at[0])
    load_o2 = pltpu.make_async_copy(o2_hbm.at[r], o2_v, loc.at[1])
    load_t2 = pltpu.make_async_copy(t2_hbm.at[0], t2_v, loc.at[2])
    load_i2 = pltpu.make_async_copy(i2_hbm.at[0], i2_v.at[h], loc.at[3])
    load_i1 = pltpu.make_async_copy(i1_hbm.at[0], i1_v.at[h], loc.at[4])
    load_a = pltpu.make_async_copy(a_hbm.at[0], a_v, loc.at[5])
    load_t1 = pltpu.make_async_copy(t1_hbm.at[0], t1_v, loc.at[15])
    for load in (*load_labels, load_o1, load_o2, load_i1, load_a, load_i2, load_t2, load_t1):
        load.start()

    load_o1.wait()
    load_o2.wait()
    low8 = lax.broadcasted_iota(jnp.int32, (8, 128), 1) < 64
    even = o1_v[pl.ds(0, 8, stride=2), :]
    odd = o1_v[pl.ds(1, 8, stride=2), :]
    shift = jnp.where(low8, 0, 128)
    skel = jnp.where(low8, even, pltpu.roll(odd, 64, 1)) + shift
    redu = jnp.where(low8, pltpu.roll(even, 64, 1), odd) + shift
    base = pl.multiple_of(c * 8, 8)
    mine2 = o2_v[pl.ds(base, 8), :]
    theirs2 = o2_v[pl.ds(pl.multiple_of(8 - base, 8), 8), :]
    theirs2 = jnp.where(h == 0, theirs2, pltpu.roll(theirs2, 4, 0))
    comp = jnp.take_along_axis(skel, mine2, axis=1, mode="promise_in_bounds")
    columns = jnp.concatenate([comp, redu, mine2], axis=0).astype(F32).T
    comp_own = jnp.where(h == 0, comp, pltpu.roll(comp, 4, 0))
    redu_own = jnp.where(h == 0, redu, pltpu.roll(redu, 4, 0))
    wide = lax.broadcasted_iota(jnp.int32, (128, 256), 1).astype(F32)
    tall = lax.broadcasted_iota(jnp.int32, (256, 128), 0)
    square = lax.broadcasted_iota(jnp.int32, (128, 128), 0)
    low64 = lax.broadcasted_iota(jnp.int32, (64, 128), 1) < 64
    low128 = lax.broadcasted_iota(jnp.int32, (128, 128), 1) < 64
    low256 = lax.broadcasted_iota(jnp.int32, (256, 128), 1) < 64
    low512 = lax.broadcasted_iota(jnp.int32, (512, 128), 1) < 64

    def onehot(rows, index):
        return jnp.where(rows == index, 1.0, 0.0).astype(BF16)

    for k in range(8):
        xt[k, 0:128, :] = onehot(wide, columns[:, k : k + 1])
        xt[k, 128:256, :] = onehot(wide, columns[:, 8 + k : 9 + k])
    for i in range(4):
        row = comp_own[i : i + 1, :]
        yk[i, :, 0:128] = onehot(tall, pltpu.roll(row, 64, 1) if i % 2 else row)
        row = theirs2[i : i + 1, :]
        p2x[i] = onehot(square, pltpu.roll(row, 64, 1) if i % 2 else row)

    def packed(ref, hs, q):
        return jnp.concatenate([ref[hs, 2 * q], ref[hs, 2 * q + 1]], axis=1)

    def fold_inverse(hs, i, index):
        pack = packed(i1_v, hs, i)
        diag = jnp.concatenate([jnp.where(low64, pack, 0.0), jnp.where(low64, 0.0, pack)], axis=0)
        both = jnp.concatenate(halves(diag), axis=1)
        return dot(onehot(tall, redu_own[index : index + 1, :]), both).astype(BF16)

    def select_rows(m_ref, hs):
        for i in range(4):
            block = dot(xt[hs * 4 + i], m_ref[256 * i : 256 * i + 256, :])
            ms[0, 64 * i : 64 * i + 64, :] = block[0:64, :].astype(BF16)
            ms[1, 64 * i : 64 * i + 64, :] = block[64:128, :].astype(BF16)
            mu[128 * i : 128 * i + 128, :] = block[128:256, :].astype(BF16)

    def select_cols(rho, hs):
        part = []
        for i in range(4):
            both = dot(ms[rho, :, 256 * i : 256 * i + 256], yk[i])
            part.append(both[:, 0:128])
            sr[rho, hs, :, 128 * i : 128 * i + 128] = (both[:, 128:256] + both[:, 256:384]).astype(BF16)
        for q in range(2):
            e_t, o_t = part[2 * q], part[2 * q + 1]
            ks[rho, hs, :, 128 * q : 128 * q + 128] = jnp.where(low256, e_t, o_t).astype(BF16)
            ks[rho, hs, :, 256 + 128 * q : 384 + 128 * q] = jnp.where(low256, o_t, e_t).astype(BF16)

    def select_lower(hs):
        part = [dot(mu[:, 256 * i : 256 * i + 256], yk[i, :, 0:128]) for i in range(4)]
        for q in range(2):
            e_t, o_t = part[2 * q], part[2 * q + 1]
            u1[hs, :, 128 * q : 128 * q + 128] = jnp.where(low512, e_t, o_t).astype(BF16)
            u1[hs, :, 256 + 128 * q : 384 + 128 * q] = jnp.where(low512, o_t, e_t).astype(BF16)

    pl.semaphore_wait(barrier, 2)
    load_i2.wait()
    send_t1 = to_k(t1_hbm.at[0], t1_in, 0)
    send_i1 = to_k(i1_hbm.at[0], i1_v.at[h], 1)
    send_i2 = to_k(i2_hbm.at[0], i2_v.at[h], 2)
    send_i2.start()
    send_t1.start()
    send_i1.start()

    for load in load_labels:
        load.wait()
    lane = lax.broadcasted_iota(jnp.int32, (1, 128), 1)
    prev1, last1 = chain_table(rows1, cols1, count1, 8, lane)
    prev2, last2 = chain_table(rows2, cols2, count2, 4, lane)
    tab[0:1, :] = prev1
    tab[1:2, :] = last1
    tab[2:3, :] = prev2
    tab[3:4, :] = last2
    tab[4:8, :] = jnp.zeros((4, 128), jnp.int32)
    send_tab_k = to_k(tab, tab_k, 3)
    send_tab_k.start()
    send_tab_x = to_x(tab, tab_x, 0)
    send_tab_x.start()
    own_tab = pltpu.make_async_copy(tab, own_s, loc.at[6])
    own_tab.start()

    load_i1.wait()
    for i in range(4):
        yk[i, :, 128:384] = fold_inverse(h, i, i)
    load_a.wait()
    select_rows(a_v, h)
    select_cols(0, h)
    send_sr0 = to_k(sr.at[0, h], spart.at[0, h], 4)
    send_sr0.start()
    select_cols(1, h)
    send_sr1 = to_k(sr.at[1, h], spart.at[1, h], 5)
    send_sr1.start()
    select_lower(h)

    send_i2.wait_recv()
    for k in range(8):
        high, rest = halves(i2_v[k // 4, k % 4])
        both = jnp.concatenate([high, rest], axis=0)
        p2 = onehot(wide[:, 0:128], columns[:, 16 + k : 17 + k])
        p2l[k, 0:64, :] = p2[0:64, :]
        p2l[k, 64:192, :] = dot(both, p2[64:128, :]).astype(BF16)
    load_t2.wait()
    own_tab.wait()
    acco[0] = jnp.zeros((128, 128), F32)
    sends_q = []
    for n in range(NT):
        half = dot(t2_v[n], p2x[cols2[0, n]]).astype(BF16)
        tile = dot(p2l[rows2[0, n]], half)
        top, bottom = tile[0:64, :], tile[64:128, :] + tile[128:192, :]
        is_even = (cols2[0, n] & 1) == 0
        xq[n] = jnp.where(low64 == is_even, bottom, top).astype(BF16)
        before = own_s[2, n]
        acco[n + 1, 0:64, :] = top + acco[before, 0:64, :]
        acco[n + 1, 64:128, :] = bottom + acco[before, 64:128, :]
        if n % 4 == 3:
            part = pl.ds(n - 3, 4)
            sends_q.append(to_x(xq.at[part], xq_in.at[part], 1 + n // 4))
            sends_q[-1].start()

    def place(acc, acc16, tiles, table, dst):
        acc[0] = jnp.zeros((128, 128), F32)
        acc16[0] = jnp.zeros((128, 128), BF16)
        for n in range(NT):
            total = tiles[n].astype(F32) + acc[table[0, n]]
            acc[n + 1] = total
            acc16[n + 1] = total.astype(BF16)
        for i in range(8):
            for j in range(8):
                dst[128 * i : 128 * i + 128, 128 * j : 128 * j + 128] = acc16[table[1, 8 * i + j]]

    load_t1.wait()
    send_i1.wait_recv()
    for i in range(4):
        orp[i] = fold_inverse(other, i, 4 + i)
    place(accb, accb16, t1_v, own_s, b_v)
    for i in range(4):
        block = dot(xt[h * 4 + i, 0:128, :], b_v[256 * i : 256 * i + 256, :]).astype(BF16)
        ms[0, 64 * i : 64 * i + 64, :] = block[0:64, :]
        ms[1, 64 * i : 64 * i + 64, :] = block[64:128, :]
    for rho in range(2):
        for i in range(4):
            both = dot(ms[rho, :, 256 * i : 256 * i + 256], orp[i])
            spart[rho, h, :, 128 * i : 128 * i + 128] = (both[:, 0:128] + both[:, 128:256]).astype(BF16)

    send_t1.wait_recv()
    send_tab_k.wait_recv()
    k_tab = pltpu.make_async_copy(tab_k, k_s, loc.at[7])
    k_tab.start()
    k_tab.wait()
    place(acca, acca16, t1_in, k_s, c_v)
    select_rows(c_v, other)
    select_lower(other)
    select_cols(0, other)

    send_sr0.wait_recv()
    sends_l = []
    for hs in range(2):
        own = dot(sr[0, hs], u1[h, :, 256:512])
        far = dot(spart[0, hs], u1[other, :, 256:512])
        lsr[hs] = (ks[0, hs, :, 256:512].astype(F32) - own - far).astype(BF16)
        sends_l.append(to_k(lsr.at[hs], lsr_in.at[hs], 6 + hs))
        sends_l[-1].start()

    for i in range(8):
        hs, i4 = i // 4, i % 4
        for q in range(2):
            e_t = acco[own_s[3, 4 * i + 2 * q]]
            o_t = acco[own_s[3, 4 * i + 2 * q + 1]]
            s_cols = jnp.where(low128, e_t, o_t)
            lanes = slice(128 * q, 128 * q + 128)
            bss[64 * i : 64 * i + 64, lanes] = s_cols[0:64, :]
            swap = 64 * (i4 ^ 1)
            vown[hs, swap : swap + 64, lanes] = s_cols[64:128, :].astype(BF16)
            bsr[64 * i : 64 * i + 64, lanes] = jnp.where(low64, o_t[0:64, :], e_t[0:64, :]).astype(BF16)
    send_bsr = to_k(bsr, bsr_in, 8)
    send_bsr.start()

    sends_p = []
    for hs in range(2):
        sends_l[hs].wait_recv()
        for m in range(2):
            at = 256 * hs + 128 * m
            rows = slice(128 * m, 128 * m + 128)
            total = bss[at : at + 128, :] - dot(lsr[hs, rows, :], vown[h]) - dot(lsr_in[hs, rows, :], vown[other])
            p_out[at : at + 128, :] = total.astype(BF16)
            part = pl.ds(at, 128)
            sends_p.append(to_x(p_out.at[part], p_in.at[part], 5 + 2 * hs + m))
            sends_p[-1].start()

    send_tab_x.wait_recv()
    x_tab = pltpu.make_async_copy(tab_x, x_s, loc.at[8])
    x_tab.start()
    x_tab.wait()
    for send in sends_q:
        send.wait_recv()
    accx[0] = jnp.zeros((64, 128), F32)
    for n in range(NT):
        accx[n + 1] = xq_in[n].astype(F32) + accx[x_s[2, n]]
    for i in range(8):
        hs, i4 = i // 4, i % 4
        for q in range(2):
            e_t = accx[x_s[3, 4 * i + 2 * q]]
            o_t = accx[x_s[3, 4 * i + 2 * q + 1]]
            lanes = slice(128 * q, 128 * q + 128)
            swap = 64 * (i4 ^ 1)
            vx[hs, swap : swap + 64, lanes] = jnp.where(low64, e_t, o_t).astype(BF16)
            csr[64 * i : 64 * i + 64, lanes] = jnp.where(low64, o_t, e_t).astype(BF16)
    send_csr = to_k(csr, csr_in, 9)
    send_csr.start()

    select_cols(1, other)
    send_sr1.wait_recv()
    for hs in range(2):
        own = dot(sr[0, hs], u1[h, :, 0:256])
        far = dot(spart[0, hs], u1[other, :, 0:256])
        lss[hs] = ks[0, hs, :, 0:256].astype(F32) - own - far
        own = dot(sr[1, hs], u1[h, :, 0:256])
        far = dot(spart[1, hs], u1[other, :, 0:256])
        high, rest = halves(ks[1, hs, :, 0:256].astype(F32) - own - far)
        for q in range(2):
            pack = packed(i2_v, hs, q)
            anti = jnp.concatenate([jnp.where(low64, 0.0, pack), jnp.where(low64, pack, 0.0)], axis=0)
            a_high, a_rest = halves(anti)
            rows = slice(128 * q, 128 * q + 128)
            total = dot(a_high, high[rows, :]) + dot(a_rest, high[rows, :]) + dot(a_high, rest[rows, :])
            uu[hs, rows, :] = total.astype(BF16)

    send_bsr.wait_recv()
    top = pl.multiple_of(c * 512, 512)
    bottom = pl.multiple_of(512 - c * 512, 512)
    for hs in range(2):
        rows = slice(256 * hs, 256 * hs + 256)
        total = lss[hs] - dot(lsr[hs], uu[h]) - dot(lsr_in[hs], uu[other])
        total = total - dot(bsr[rows, :], vx[h]) - dot(bsr_in[rows, :], vx[other])
        out_ref[0, pl.ds(top + 256 * hs, 256), :] = total.astype(BF16)
    send_csr.wait_recv()
    for hs in range(2):
        rows = slice(256 * hs, 256 * hs + 256)
        lss[hs] = dot(csr[rows, :], uu[h]) + dot(csr_in[rows, :], uu[other])
    for m in range(4):
        at = 128 * m
        rows = slice(128 * (m % 2), 128 * (m % 2) + 128)
        sends_p[m].wait_recv()
        total = p_in[at : at + 128, :].astype(F32) - lss[m // 2, rows, :]
        out_ref[0, pl.ds(bottom + at, 128), :] = total.astype(BF16)

    for send in (send_t1, send_i1, send_i2, send_tab_k, send_tab_x, send_sr0, send_sr1, *sends_q, *sends_l, send_bsr, *sends_p, send_csr):
        send.wait_send()


def local(*args):
    schur, t1, rows1, cols1, count1, o1, i1, t2, rows2, cols2, count2, o2, i2 = args
    hbm = pl.BlockSpec(memory_space=pltpu.HBM)
    label = pltpu.SMEM((1, 16), jnp.int32)
    count = pltpu.SMEM((1,), jnp.int32)
    vmem = pltpu.VMEM
    table = vmem((8, 128), jnp.int32)
    table_s = pltpu.SMEM((8, 128), jnp.int32)
    matrix = vmem((1024, 1024), BF16)
    tiles = vmem((16, 128, 128), BF16)
    panel = vmem((512, 256), BF16)
    panels = vmem((2, 256, 256), BF16)
    dma = pltpu.SemaphoreType.DMA
    scratch = [
        label, label, count, label, label, count,
        matrix, matrix, matrix, tiles, tiles, tiles,
        vmem((2, 8, 64, 64), F32), vmem((2, 4, 64, 64), F32), vmem((16, 128), jnp.int32), vmem((16, 128), jnp.int32),
        table, table, table, table_s, table_s, table_s,
        vmem((8, 256, 256), BF16), vmem((4, 256, 384), BF16), vmem((4, 256, 256), BF16),
        vmem((8, 192, 128), BF16), vmem((4, 128, 128), BF16),
        vmem((17, 128, 128), F32), vmem((17, 128, 128), F32), vmem((17, 128, 128), F32), vmem((17, 64, 128), F32),
        vmem((17, 128, 128), BF16), vmem((17, 128, 128), BF16),
        vmem((16, 64, 128), BF16), vmem((16, 64, 128), BF16),
        vmem((2, 256, 1024), BF16), vmem((512, 1024), BF16), vmem((2, 2, 256, 512), BF16), vmem((2, 512, 512), BF16),
        vmem((2, 2, 256, 512), BF16), vmem((2, 2, 256, 512), BF16),
        vmem((2, 256, 256), F32), panels, panels, panels, panels, panels,
        vmem((512, 256), F32), panel, panel, panel, panel, panel, panel,
        dma((16,)), dma((10,)), dma((10,)), dma((9,)), dma((9,)),
    ]
    large = [pltpu.with_memory_space_constraint(x, pltpu.HBM) for x in (schur, t1, t2, i1, i2, o1, o2)]
    return pl.pallas_call(
        kernel,
        out_shape=pltpu.VMEM((1, 1024, 256), BF16),
        in_specs=[hbm] * 13,
        out_specs=pl.BlockSpec(memory_space=pltpu.VMEM),
        scratch_shapes=scratch,
        compiler_params=pltpu.CompilerParams(collective_id=0, has_side_effects=True, vmem_limit_bytes=62 * 2**20),
    )(*large, rows1, cols1, count1, rows2, cols2, count2)


def solution(mesh):
    boxes = ("leaf", "blk")
    return jax.shard_map(
        local,
        mesh=mesh,
        in_specs=(
            P(boxes, None, None),
            P(boxes, None, None, None),
            P(boxes, None),
            P(boxes, None),
            P(boxes),
            P(),
            P(boxes, None, None, None),
            P(boxes, None, None, None),
            P(boxes, None),
            P(boxes, None),
            P(boxes),
            P(),
            P(boxes, None, None, None),
        ),
        out_specs=P(boxes, None, None),
        check_vma=False,
    )
```

```python
import jax
import jax.numpy as jnp
from jax import lax
from jax.experimental import pallas as pl
from jax.experimental.pallas import tpu as pltpu
from jax.sharding import PartitionSpec as P

MESH = pl.DeviceIdType.MESH
F32 = jnp.float32
BF16 = jnp.bfloat16
NT = 16


def dot(a, b):
    return jnp.dot(a, b, preferred_element_type=F32)


def chain_table(rows, cols, count, halved, lane):
    live = count[0]
    targets = [rows[0, n] * 4 + (cols[0, n] >> halved) for n in range(NT)]
    along = jnp.full((1, 128), -1, jnp.int32)
    columns = jnp.zeros((1, 128), jnp.int32)
    for n in range(NT):
        along = jnp.where(lane == n, targets[n], along)
        columns = jnp.where(lane == n, cols[0, n], columns)
    prev = jnp.zeros((1, 128), jnp.int32)
    last = jnp.zeros((1, 128), jnp.int32)
    for n in range(NT):
        value = jnp.where(n < live, n + 1, 0)
        prev = jnp.maximum(prev, jnp.where((along == targets[n]) & (lane > n), value, 0))
        last = jnp.maximum(last, jnp.where(lane == targets[n], value, 0))
    return prev, last, columns


def halves(value):
    high = value.astype(BF16)
    return high, (value - high.astype(F32)).astype(BF16)


def kernel(
    a_hbm, t1_hbm, t2_hbm, i1_hbm, i2_hbm, o1_hbm, o2_hbm,
    rows1_hbm, cols1_hbm, count1_hbm, rows2_hbm, cols2_hbm, count2_hbm,
    out_ref,
    rows1, cols1, count1, rows2, cols2, count2,
    a_v, t1_v, t1_in, t2_v, i1_v, i2_v, o1_v, o2_v,
    tab, tab_k, tab_x, own_s, k_s, x_s,
    xt, yk, orp, p2s, p2v, p2x,
    accb, accc, acct, accv, accxs, accxv, halfs, srq, srq_in, vq, vq_in,
    amc, ame, ks, u1, sr, spart,
    lss, lsr, lsr_in, uu, vown, vx,
    bss, bsr, bsr_in, csr, csr_in, p_out, p_in,
    loc, ksend, krecv, xsend, xrecv,
):
    leaf = lax.axis_index("leaf")
    c = lax.axis_index("blk")
    r = leaf // 2
    h = leaf - 2 * r
    other = 1 - h
    kid = {"leaf": leaf + 1 - 2 * h}
    xid = {"blk": 1 - c}

    def to_k(src, dst, n):
        return pltpu.make_async_remote_copy(
            src_ref=src, dst_ref=dst, send_sem=ksend.at[n], recv_sem=krecv.at[n],
            device_id=kid, device_id_type=MESH,
        )

    def to_x(src, dst, n):
        return pltpu.make_async_remote_copy(
            src_ref=src, dst_ref=dst, send_sem=xsend.at[n], recv_sem=xrecv.at[n],
            device_id=xid, device_id_type=MESH,
        )

    barrier = pltpu.get_barrier_semaphore()
    pl.semaphore_signal(barrier, inc=1, device_id=xid, device_id_type=MESH)
    pl.semaphore_signal(barrier, inc=1, device_id=kid, device_id_type=MESH)

    pairs = (
        (rows2_hbm, rows2), (cols2_hbm, cols2), (count2_hbm, count2),
        (rows1_hbm, rows1), (cols1_hbm, cols1), (count1_hbm, count1),
    )
    load_labels = [pltpu.make_async_copy(src, dst, loc.at[9 + n]) for n, (src, dst) in enumerate(pairs)]
    load_o1 = pltpu.make_async_copy(o1_hbm.at[2 * r + c], o1_v, loc.at[0])
    load_o2 = pltpu.make_async_copy(o2_hbm.at[r], o2_v, loc.at[1])
    load_t2 = pltpu.make_async_copy(t2_hbm.at[0], t2_v, loc.at[2])
    load_i2 = pltpu.make_async_copy(i2_hbm.at[0], i2_v.at[h], loc.at[3])
    load_i1 = pltpu.make_async_copy(i1_hbm.at[0], i1_v.at[h], loc.at[4])
    load_a = pltpu.make_async_copy(a_hbm.at[0], a_v, loc.at[5])
    load_t1 = pltpu.make_async_copy(t1_hbm.at[0], t1_v, loc.at[15])
    for load in (load_o2, *load_labels, load_t2, load_o1, load_i1, load_a, load_i2, load_t1):
        load.start()

    wide = lax.broadcasted_iota(jnp.int32, (128, 256), 1).astype(F32)
    tall = lax.broadcasted_iota(jnp.int32, (256, 128), 0)
    square = lax.broadcasted_iota(jnp.int32, (128, 128), 0)
    low8 = lax.broadcasted_iota(jnp.int32, (8, 128), 1) < 64
    low64 = lax.broadcasted_iota(jnp.int32, (64, 128), 1) < 64
    low256 = lax.broadcasted_iota(jnp.int32, (256, 128), 1) < 64
    lane = lax.broadcasted_iota(jnp.int32, (1, 128), 1)

    def onehot(rows, index):
        return jnp.where(rows == index, 1.0, 0.0).astype(BF16)

    load_o2.wait()
    base = pl.multiple_of(c * 8, 8)
    mine2 = o2_v[pl.ds(base, 8), :]
    theirs2 = o2_v[pl.ds(pl.multiple_of(8 - base, 8), 8), :]
    theirs2 = jnp.where(h == 0, theirs2, pltpu.roll(theirs2, 4, 0))
    columns2 = mine2.astype(F32).T
    for i in range(4):
        row = theirs2[i : i + 1, :]
        p2x[i] = onehot(square, pltpu.roll(row, 64, 1) if i % 2 else row)
    for k in range(8):
        p2s[k] = onehot(wide[:, 0:128], columns2[:, k : k + 1])

    for load in load_labels:
        load.wait()
    prev1, last1, cols_row1 = chain_table(rows1, cols1, count1, 1, lane)
    prev2, last2, cols_row2 = chain_table(rows2, cols2, count2, 0, lane)
    tab[0:1, :] = prev1
    tab[1:2, :] = last1
    tab[2:3, :] = prev2
    tab[3:4, :] = last2
    tab[4:5, :] = cols_row1
    tab[5:6, :] = cols_row2
    tab[6:8, :] = jnp.zeros((2, 128), jnp.int32)
    own_tab = pltpu.make_async_copy(tab, own_s, loc.at[6])
    own_tab.start()

    pl.semaphore_wait(barrier, 2)
    send_t1 = to_k(t1_hbm.at[0], t1_in, 0)
    send_i1 = to_k(i1_hbm.at[0], i1_v.at[h], 1)
    send_i2 = to_k(i2_hbm.at[0], i2_v.at[h], 2)
    send_tab_k = to_k(tab, tab_k, 3)
    send_tab_x = to_x(tab, tab_x, 0)
    for send in (send_i2, send_i1, send_t1, send_tab_k, send_tab_x):
        send.start()

    def turned(value, column, wanted):
        return jnp.where((column & 1) == wanted, pltpu.roll(value, 64, 1), value)

    load_t2.wait()
    own_tab.wait()
    acct[0] = jnp.zeros((64, 128), BF16)
    accv[0] = jnp.zeros((64, 128), BF16)
    sends_q = []
    tops = []
    order = [n for m in range(8) for n in (m, m + 8)]
    for n in order:
        half = dot(t2_v[n], p2x[cols2[0, n]]).astype(BF16)
        halfs[n] = half
        top = dot(p2s[rows2[0, n], 0:64, :], half)
        acct[n + 1] = top.astype(BF16)
        tops.append(turned(top, cols2[0, n], n // 8))
        if n >= 8:
            srq[n - 8] = jnp.where(low64, tops[-2], tops[-1]).astype(BF16)
        if n in (11, 15):
            part = pl.ds(n - 11, 4)
            sends_q.append(to_x(srq.at[part], srq_in.at[part], 1 + (n - 11) // 4))
            sends_q[-1].start()

    load_o1.wait()
    even = o1_v[pl.ds(0, 8, stride=2), :]
    odd = o1_v[pl.ds(1, 8, stride=2), :]
    shift = jnp.where(low8, 0, 128)
    skel = jnp.where(low8, even, pltpu.roll(odd, 64, 1)) + shift
    redu = jnp.where(low8, pltpu.roll(even, 64, 1), odd) + shift
    comp = jnp.take_along_axis(skel, mine2, axis=1, mode="promise_in_bounds")
    columns = jnp.concatenate([comp, redu], axis=0).astype(F32).T
    comp_own = jnp.where(h == 0, comp, pltpu.roll(comp, 4, 0))
    redu_own = jnp.where(h == 0, redu, pltpu.roll(redu, 4, 0))
    for k in range(8):
        xt[k, 0:128, :] = onehot(wide, columns[:, k : k + 1])
        xt[k, 128:256, :] = onehot(wide, columns[:, 8 + k : 9 + k])

    def packed(ref, hs, q):
        return jnp.concatenate([ref[hs, 2 * q], ref[hs, 2 * q + 1]], axis=1)

    def fold_inverse(hs, i, index):
        pack = packed(i1_v, hs, i)
        diag = jnp.concatenate([jnp.where(low64, pack, 0.0), jnp.where(low64, 0.0, pack)], axis=0)
        return dot(onehot(tall, redu_own[index : index + 1, :]), diag.astype(BF16)).astype(BF16)

    load_i1.wait()
    for i in range(4):
        row = comp_own[i : i + 1, :]
        skeleton = onehot(tall, pltpu.roll(row, 64, 1) if i % 2 else row)
        weighted = fold_inverse(h, i, i)
        for m in range(2):
            yk[2 * i + m, :, 0:128] = skeleton[128 * m : 128 * m + 128, :]
            yk[2 * i + m, :, 128:256] = weighted[128 * m : 128 * m + 128, :]

    def select_rows(read, read_e, hs):
        for i in range(4):
            block = dot(xt[hs * 4 + i], read(i))
            panel = dot(xt[hs * 4 + i, 0:128, :], read_e(i)).astype(BF16)
            rows = slice(64 * i, 64 * i + 64)
            for q in range(2):
                e_t, o_t = block[:, 256 * q : 256 * q + 128], block[:, 256 * q + 128 : 256 * q + 256]
                s_cols = jnp.where(low256, e_t, o_t).astype(BF16)
                r_cols = jnp.where(low256, o_t, e_t).astype(BF16)
                s_at = slice(128 * q, 128 * q + 128)
                r_at = slice(256 + 128 * q, 384 + 128 * q)
                ks[0, hs, rows, s_at] = s_cols[0:64, :]
                ks[1, hs, rows, s_at] = s_cols[64:128, :]
                ks[0, hs, rows, r_at] = r_cols[0:64, :]
                u1[hs, 128 * i : 128 * i + 128, s_at] = s_cols[128:256, :]
                u1[hs, 128 * i : 128 * i + 128, r_at] = r_cols[128:256, :]
            sr[0, hs, rows, :] = panel[0:64, :]
            sr[1, hs, rows, :] = panel[64:128, :]

    load_a.wait()
    for i in range(4):
        weights = yk[2 * i : 2 * i + 2].reshape(256, 256)
        both = dot(a_v[:, 256 * i : 256 * i + 256], weights).astype(BF16)
        amc[:, 128 * i : 128 * i + 128] = both[:, 0:128]
        ame[:, 128 * i : 128 * i + 128] = both[:, 128:256]
    select_rows(lambda i: amc[256 * i : 256 * i + 256, :], lambda i: ame[256 * i : 256 * i + 256, :], h)
    send_sr = to_k(sr.at[:, h], spart.at[:, h], 4)
    send_sr.start()

    load_i2.wait()
    send_i2.wait_recv()
    for k in range(8):
        both = jnp.concatenate(halves(i2_v[k // 4, k % 4]), axis=0)
        p2v[k] = dot(both, p2s[k, 64:128, :]).astype(BF16)
    bottoms = []
    for n in order:
        both = dot(p2v[rows2[0, n]], halfs[n])
        bottom = both[0:64, :] + both[64:128, :]
        accv[n + 1] = bottom.astype(BF16)
        bottoms.append(turned(bottom, cols2[0, n], 1 - n // 8))
        if n >= 8:
            vq[n - 8] = jnp.where(low64, bottoms[-2], bottoms[-1]).astype(BF16)
        if n in (11, 15):
            part = pl.ds(n - 11, 4)
            sends_q.append(to_x(vq.at[part], vq_in.at[part], 3 + (n - 11) // 4))
            sends_q[-1].start()

    def link(acc, n, before, value):
        acc[n + 1] = (value + acc[before].astype(F32)).astype(BF16)

    def coupling(acc, table, lanes):
        def read(i):
            blocks = [[acc[table[1, 4 * j + m], :, lanes] for m in range(4)] for j in (2 * i, 2 * i + 1)]
            return jnp.concatenate([jnp.concatenate(row, axis=1) for row in blocks], axis=0)

        return read

    load_t1.wait()
    send_i1.wait_recv()
    for i in range(4):
        weighted = fold_inverse(other, i, 4 + i)
        for m in range(2):
            orp[2 * i + m] = weighted[128 * m : 128 * m + 128, :]
    accb[0] = jnp.zeros((128, 128), BF16)
    for n in range(NT):
        link(accb, n, own_s[0, n], dot(t1_v[n], orp[cols1[0, n]]))
    read = coupling(accb, own_s, slice(0, 128))
    for i in range(4):
        panel = dot(xt[h * 4 + i, 0:128, :], read(i)).astype(BF16)
        spart[0, h, 64 * i : 64 * i + 64, :] = panel[0:64, :]
        spart[1, h, 64 * i : 64 * i + 64, :] = panel[64:128, :]

    send_t1.wait_recv()
    send_tab_k.wait_recv()
    k_tab = pltpu.make_async_copy(tab_k, k_s, loc.at[7])
    k_tab.start()
    k_tab.wait()
    accc[0] = jnp.zeros((128, 256), BF16)
    for n in range(NT):
        link(accc, n, k_s[0, n], dot(t1_in[n], yk[k_s[4, n]]))
    select_rows(coupling(accc, k_s, slice(0, 128)), coupling(accc, k_s, slice(128, 256)), other)

    send_sr.wait_recv()
    sends_l = []
    for hs in range(2):
        own = dot(sr[0, hs], u1[h, :, 256:512])
        far = dot(spart[0, hs], u1[other, :, 256:512])
        lsr[hs] = (ks[0, hs, :, 256:512].astype(F32) - own - far).astype(BF16)
        sends_l.append(to_k(lsr.at[hs], lsr_in.at[hs], 5 + hs))
        sends_l[-1].start()

    for n in range(NT):
        before = own_s[2, n]
        link(acct, n, before, acct[n + 1].astype(F32))
        link(accv, n, before, accv[n + 1].astype(F32))
    for i in range(8):
        hs, i4 = i // 4, i % 4
        for q in range(2):
            e_at, o_at = own_s[3, 4 * i + 2 * q], own_s[3, 4 * i + 2 * q + 1]
            lanes = slice(128 * q, 128 * q + 128)
            swap = 64 * (i4 ^ 1)
            bss[64 * i : 64 * i + 64, lanes] = jnp.where(low64, acct[e_at], acct[o_at])
            bsr[64 * i : 64 * i + 64, lanes] = jnp.where(low64, acct[o_at], acct[e_at])
            vown[hs, swap : swap + 64, lanes] = jnp.where(low64, accv[e_at], accv[o_at])
    send_bsr = to_k(bsr, bsr_in, 7)
    send_bsr.start()

    for hs in range(2):
        own = dot(sr[0, hs], u1[h, :, 0:256])
        far = dot(spart[0, hs], u1[other, :, 0:256])
        lss[hs] = ks[0, hs, :, 0:256].astype(F32) - own - far

    sends_p = []
    for hs in range(2):
        sends_l[hs].wait_recv()
        for m in range(2):
            at = 256 * hs + 128 * m
            rows = slice(128 * m, 128 * m + 128)
            total = bss[at : at + 128, :].astype(F32) - dot(lsr[hs, rows, :], vown[h]) - dot(lsr_in[hs, rows, :], vown[other])
            p_out[at : at + 128, :] = total.astype(BF16)
            part = pl.ds(at, 128)
            sends_p.append(to_x(p_out.at[part], p_in.at[part], 5 + 2 * hs + m))
            sends_p[-1].start()

    send_tab_x.wait_recv()
    x_tab = pltpu.make_async_copy(tab_x, x_s, loc.at[8])
    x_tab.start()
    x_tab.wait()
    for send in sends_q:
        send.wait_recv()
    accxs[0] = jnp.zeros((64, 128), BF16)
    accxv[0] = jnp.zeros((64, 128), BF16)
    for n in range(NT):
        link(accxs, n, x_s[2, n], turned(srq_in[n % 8].astype(F32), x_s[5, n], n // 8))
        link(accxv, n, x_s[2, n], turned(vq_in[n % 8].astype(F32), x_s[5, n], 1 - n // 8))
    for i in range(8):
        hs, i4 = i // 4, i % 4
        for q in range(2):
            e_at, o_at = x_s[3, 4 * i + 2 * q], x_s[3, 4 * i + 2 * q + 1]
            lanes = slice(128 * q, 128 * q + 128)
            swap = 64 * (i4 ^ 1)
            vx[hs, swap : swap + 64, lanes] = jnp.where(low64, accxv[e_at], accxv[o_at])
            csr[64 * i : 64 * i + 64, lanes] = jnp.where(low64, accxs[o_at], accxs[e_at])
    send_csr = to_k(csr, csr_in, 8)
    send_csr.start()

    for hs in range(2):
        own = dot(sr[1, hs], u1[h, :, 0:256])
        far = dot(spart[1, hs], u1[other, :, 0:256])
        high, rest = halves(ks[1, hs, :, 0:256].astype(F32) - own - far)
        for q in range(2):
            pack = packed(i2_v, hs, q)
            anti = jnp.concatenate([jnp.where(low64, 0.0, pack), jnp.where(low64, pack, 0.0)], axis=0)
            a_high, a_rest = halves(anti)
            rows = slice(128 * q, 128 * q + 128)
            total = dot(a_high, high[rows, :]) + dot(a_rest, high[rows, :]) + dot(a_high, rest[rows, :])
            uu[hs, rows, :] = total.astype(BF16)

    send_bsr.wait_recv()
    top = pl.multiple_of(c * 512, 512)
    bottom = pl.multiple_of(512 - c * 512, 512)
    for hs in range(2):
        rows = slice(256 * hs, 256 * hs + 256)
        total = lss[hs] - dot(lsr[hs], uu[h]) - dot(lsr_in[hs], uu[other])
        total = total - dot(bsr[rows, :], vx[h]) - dot(bsr_in[rows, :], vx[other])
        out_ref[0, pl.ds(top + 256 * hs, 256), :] = total.astype(BF16)
    send_csr.wait_recv()
    for hs in range(2):
        rows = slice(256 * hs, 256 * hs + 256)
        lss[hs] = dot(csr[rows, :], uu[h]) + dot(csr_in[rows, :], uu[other])
    for m in range(4):
        at = 128 * m
        rows = slice(128 * (m % 2), 128 * (m % 2) + 128)
        sends_p[m].wait_recv()
        total = p_in[at : at + 128, :].astype(F32) - lss[m // 2, rows, :]
        out_ref[0, pl.ds(bottom + at, 128), :] = total.astype(BF16)

    for send in (send_t1, send_i1, send_i2, send_tab_k, send_tab_x, send_sr, *sends_q, *sends_l, send_bsr, *sends_p, send_csr):
        send.wait_send()


def local(*args):
    schur, t1, rows1, cols1, count1, o1, i1, t2, rows2, cols2, count2, o2, i2 = args
    hbm = pl.BlockSpec(memory_space=pltpu.HBM)
    label = pltpu.SMEM((1, 16), jnp.int32)
    count = pltpu.SMEM((1,), jnp.int32)
    vmem = pltpu.VMEM
    table = vmem((8, 128), jnp.int32)
    table_s = pltpu.SMEM((8, 128), jnp.int32)
    tiles = vmem((16, 128, 128), BF16)
    panel = vmem((512, 256), BF16)
    panels = vmem((2, 256, 256), BF16)
    onehots = vmem((8, 128, 128), BF16)
    chained = vmem((17, 64, 128), BF16)
    quads = vmem((8, 64, 128), BF16)
    dma = pltpu.SemaphoreType.DMA
    scratch = [
        label, label, count, label, label, count,
        vmem((1024, 1024), BF16), tiles, tiles, tiles,
        vmem((2, 8, 64, 64), F32), vmem((2, 4, 64, 64), F32), vmem((16, 128), jnp.int32), vmem((16, 128), jnp.int32),
        table, table, table, table_s, table_s, table_s,
        vmem((8, 256, 256), BF16), vmem((8, 128, 256), BF16), onehots, onehots, onehots, vmem((4, 128, 128), BF16),
        vmem((17, 128, 128), BF16), vmem((17, 128, 256), BF16), chained, chained, chained, chained, tiles,
        quads, quads, quads, quads,
        vmem((1024, 512), BF16), vmem((1024, 512), BF16), vmem((2, 2, 256, 512), BF16), vmem((2, 512, 512), BF16),
        vmem((2, 2, 256, 512), BF16), vmem((2, 2, 256, 512), BF16),
        vmem((2, 256, 256), F32), panels, panels, panels, panels, panels,
        panel, panel, panel, panel, panel, panel, panel,
        dma((16,)), dma((9,)), dma((9,)), dma((9,)), dma((9,)),
    ]
    large = [pltpu.with_memory_space_constraint(x, pltpu.HBM) for x in (schur, t1, t2, i1, i2, o1, o2)]
    return pl.pallas_call(
        kernel,
        out_shape=pltpu.VMEM((1, 1024, 256), BF16),
        in_specs=[hbm] * 13,
        out_specs=pl.BlockSpec(memory_space=pltpu.VMEM),
        scratch_shapes=scratch,
        compiler_params=pltpu.CompilerParams(collective_id=0, has_side_effects=True, vmem_limit_bytes=62 * 2**20),
    )(*large, rows1, cols1, count1, rows2, cols2, count2)


def solution(mesh):
    boxes = ("leaf", "blk")
    return jax.shard_map(
        local,
        mesh=mesh,
        in_specs=(
            P(boxes, None, None),
            P(boxes, None, None, None),
            P(boxes, None),
            P(boxes, None),
            P(boxes),
            P(),
            P(boxes, None, None, None),
            P(boxes, None, None, None),
            P(boxes, None),
            P(boxes, None),
            P(boxes),
            P(),
            P(boxes, None, None, None),
        ),
        out_specs=P(boxes, None, None),
        check_vma=False,
    )
```

```python
import jax
import jax.numpy as jnp
from jax import lax
from jax.experimental import pallas as pl
from jax.experimental.pallas import tpu as pltpu
from jax.sharding import PartitionSpec as P

MESH = pl.DeviceIdType.MESH
F32 = jnp.float32
BF16 = jnp.bfloat16
NT = 16


def dot(a, b):
    return jnp.dot(a, b, preferred_element_type=F32)


def chain_table(rows, cols, count, halved, lane):
    live = count[0]
    targets = [rows[0, n] * 4 + (cols[0, n] >> halved) for n in range(NT)]
    along = jnp.full((1, 128), -1, jnp.int32)
    columns = jnp.zeros((1, 128), jnp.int32)
    for n in range(NT):
        along = jnp.where(lane == n, targets[n], along)
        columns = jnp.where(lane == n, cols[0, n], columns)
    prev = jnp.zeros((1, 128), jnp.int32)
    last = jnp.zeros((1, 128), jnp.int32)
    for n in range(NT):
        value = jnp.where(n < live, n + 1, 0)
        prev = jnp.maximum(prev, jnp.where((along == targets[n]) & (lane > n), value, 0))
        last = jnp.maximum(last, jnp.where(lane == targets[n], value, 0))
    return prev, last, columns


def halves(value):
    high = value.astype(BF16)
    return high, (value - high.astype(F32)).astype(BF16)


def kernel(
    a_hbm, t1_hbm, t2_hbm, i1_hbm, i2_hbm, o1_hbm, o2_hbm,
    rows1_hbm, cols1_hbm, count1_hbm, rows2_hbm, cols2_hbm, count2_hbm,
    out_ref,
    rows1, cols1, count1, rows2, cols2, count2,
    a_v, t1_v, t1_in, t2_v, i1_v, i2_v, o1_v, o2_v,
    tab, tab_k, tab_x, own_s, k_s, x_s,
    xt, yk, orp, p2s, p2v, p2x,
    accb, accc, acct, accv, accxs, accxv, halfs, srq, srq_in, vq, vq_in,
    ams, amr, ame, ksr, kss, u1r, u1s, sr, spart,
    lss, lsr, lsr_in, uu, vown, vx,
    bss, bsr, bsr_in, csr, csr_in, p_out, p_in,
    loc, ksend, krecv, xsend, xrecv,
):
    leaf = lax.axis_index("leaf")
    c = lax.axis_index("blk")
    r = leaf // 2
    h = leaf - 2 * r
    other = 1 - h
    kid = {"leaf": leaf + 1 - 2 * h}
    xid = {"blk": 1 - c}

    def to_k(src, dst, n):
        return pltpu.make_async_remote_copy(
            src_ref=src, dst_ref=dst, send_sem=ksend.at[n], recv_sem=krecv.at[n],
            device_id=kid, device_id_type=MESH,
        )

    def to_x(src, dst, n):
        return pltpu.make_async_remote_copy(
            src_ref=src, dst_ref=dst, send_sem=xsend.at[n], recv_sem=xrecv.at[n],
            device_id=xid, device_id_type=MESH,
        )

    barrier = pltpu.get_barrier_semaphore()
    pl.semaphore_signal(barrier, inc=1, device_id=xid, device_id_type=MESH)
    pl.semaphore_signal(barrier, inc=1, device_id=kid, device_id_type=MESH)

    pairs = (
        (rows2_hbm, rows2), (cols2_hbm, cols2), (count2_hbm, count2),
        (rows1_hbm, rows1), (cols1_hbm, cols1), (count1_hbm, count1),
    )
    load_labels = [pltpu.make_async_copy(src, dst, loc.at[9 + n]) for n, (src, dst) in enumerate(pairs)]
    load_o1 = pltpu.make_async_copy(o1_hbm.at[2 * r + c], o1_v, loc.at[0])
    load_o2 = pltpu.make_async_copy(o2_hbm.at[r], o2_v, loc.at[1])
    load_t2 = pltpu.make_async_copy(t2_hbm.at[0], t2_v, loc.at[2])
    load_i2 = pltpu.make_async_copy(i2_hbm.at[0], i2_v.at[h], loc.at[3])
    load_i1 = pltpu.make_async_copy(i1_hbm.at[0], i1_v.at[h], loc.at[4])
    load_a = pltpu.make_async_copy(a_hbm.at[0], a_v, loc.at[5])
    load_t1 = pltpu.make_async_copy(t1_hbm.at[0], t1_v, loc.at[15])
    for load in (load_o2, *load_labels, load_t2, load_o1, load_i1, load_a, load_i2, load_t1):
        load.start()

    wide = lax.broadcasted_iota(jnp.int32, (128, 256), 1).astype(BF16)
    tall = lax.broadcasted_iota(jnp.int32, (256, 128), 0).astype(BF16)
    square = tall[0:128, :]
    low8 = lax.broadcasted_iota(jnp.int32, (8, 128), 1) < 64
    low64 = lax.broadcasted_iota(jnp.int32, (64, 128), 1) < 64
    low1024 = lax.broadcasted_iota(jnp.int32, (1024, 128), 1) < 64
    low128 = lax.broadcasted_iota(jnp.int32, (128, 128), 1) < 64
    lane = lax.broadcasted_iota(jnp.int32, (1, 128), 1)

    one, zero = jnp.asarray(1, BF16), jnp.asarray(0, BF16)

    def onehot(rows, index):
        return jnp.where(rows == index.astype(BF16), one, zero)

    load_o2.wait()
    base = pl.multiple_of(c * 8, 8)
    mine2 = o2_v[pl.ds(base, 8), :]
    theirs2 = o2_v[pl.ds(pl.multiple_of(8 - base, 8), 8), :]
    theirs2 = jnp.where(h == 0, theirs2, pltpu.roll(theirs2, 4, 0))
    columns2 = mine2.astype(F32).T
    for i in range(4):
        row = theirs2[i : i + 1, :]
        p2x[i] = onehot(square, pltpu.roll(row, 64, 1) if i % 2 else row)
    for k in range(8):
        p2s[k] = onehot(wide[:, 0:128], columns2[:, k : k + 1])

    for load in load_labels:
        load.wait()
    prev1, last1, cols_row1 = chain_table(rows1, cols1, count1, 1, lane)
    prev2, last2, cols_row2 = chain_table(rows2, cols2, count2, 0, lane)
    tab[0:1, :] = prev1
    tab[1:2, :] = last1
    tab[2:3, :] = prev2
    tab[3:4, :] = last2
    tab[4:5, :] = cols_row1
    tab[5:6, :] = cols_row2
    tab[6:8, :] = jnp.zeros((2, 128), jnp.int32)
    own_tab = pltpu.make_async_copy(tab, own_s, loc.at[6])
    own_tab.start()

    pl.semaphore_wait(barrier, 2)
    send_t1 = to_k(t1_hbm.at[0], t1_in, 0)
    send_i1 = to_k(i1_hbm.at[0], i1_v.at[h], 1)
    send_i2 = to_k(i2_hbm.at[0], i2_v.at[h], 2)
    send_tab_k = to_k(tab, tab_k, 3)
    send_tab_x = to_x(tab, tab_x, 0)
    for send in (send_i2, send_i1, send_t1, send_tab_k, send_tab_x):
        send.start()

    def turned(value, column, wanted):
        return jnp.where((column & 1) == wanted, pltpu.roll(value, 64, 1), value)

    load_t2.wait()
    own_tab.wait()
    acct[0] = jnp.zeros((64, 128), BF16)
    accv[0] = jnp.zeros((64, 128), BF16)
    sends_q = []
    tops = []
    order = [n for m in range(8) for n in (m, m + 8)]
    for n in order:
        half = dot(t2_v[n], p2x[cols2[0, n]]).astype(BF16)
        both = dot(p2s[rows2[0, n]], half)
        top = both[0:64, :]
        halfs[n] = both[64:128, :].astype(BF16)
        acct[n + 1] = top.astype(BF16)
        tops.append(turned(top, cols2[0, n], n // 8))
        if n >= 8:
            srq[n - 8] = jnp.where(low64, tops[-2], tops[-1]).astype(BF16)
        if n in (11, 15):
            part = pl.ds(n - 11, 4)
            sends_q.append(to_x(srq.at[part], srq_in.at[part], 1 + (n - 11) // 4))
            sends_q[-1].start()

    load_o1.wait()
    even = o1_v[pl.ds(0, 8, stride=2), :]
    odd = o1_v[pl.ds(1, 8, stride=2), :]
    shift = jnp.where(low8, 0, 128)
    skel = jnp.where(low8, even, pltpu.roll(odd, 64, 1)) + shift
    redu = jnp.where(low8, pltpu.roll(even, 64, 1), odd) + shift
    comp = jnp.take_along_axis(skel, mine2, axis=1, mode="promise_in_bounds")
    columns = jnp.concatenate([comp, redu], axis=0).astype(F32).T
    comp_own = jnp.where(h == 0, comp, pltpu.roll(comp, 4, 0))
    redu_own = jnp.where(h == 0, redu, pltpu.roll(redu, 4, 0))
    for k in range(8):
        xt[k, 0:64, :] = onehot(wide[0:64, :], columns[0:64, k : k + 1])
        xt[k, 192:256, :] = onehot(wide[64:128, :], columns[64:128, k : k + 1])
        xt[k, 64:128, 0:128] = onehot(wide[0:64, 0:128], columns[0:64, 8 + k : 9 + k])
        xt[k, 64:128, 128:256] = jnp.zeros((64, 128), BF16)
        xt[k, 128:192, 0:128] = jnp.zeros((64, 128), BF16)
        xt[k, 128:192, 128:256] = onehot(wide[0:64, 128:256], columns[64:128, 8 + k : 9 + k])

    def packed(ref, hs, q):
        return jnp.concatenate([ref[hs, 2 * q], ref[hs, 2 * q + 1]], axis=1)

    def fold_inverse(hs, i, index):
        pack = packed(i1_v, hs, i)
        diag = jnp.concatenate([jnp.where(low64, pack, 0.0), jnp.where(low64, 0.0, pack)], axis=0)
        return dot(onehot(tall, redu_own[index : index + 1, :]), diag.astype(BF16)).astype(BF16)

    load_i1.wait()
    for i in range(4):
        row = comp_own[i : i + 1, :]
        skeleton = onehot(tall, pltpu.roll(row, 64, 1) if i % 2 else row)
        weighted = fold_inverse(h, i, i)
        for m in range(2):
            yk[2 * i + m, :, 0:128] = skeleton[128 * m : 128 * m + 128, :]
            yk[2 * i + m, :, 128:256] = weighted[128 * m : 128 * m + 128, :]

    def select_first(read_r, read_e, hs):
        for i in range(4):
            block = dot(xt[hs * 4 + i, 0:192, :], read_r(i)).astype(BF16)
            rows = slice(64 * i, 64 * i + 64)
            ksr[hs, rows, :] = block[0:64, :]
            u1r[hs, 128 * i : 128 * i + 128, :] = block[64:192, :]
            sr[0, hs, rows, :] = dot(xt[hs * 4 + i, 0:64, :], read_e(i)).astype(BF16)

    def select_later(read_s, read_e, hs):
        for i in range(4):
            block = dot(xt[hs * 4 + i], read_s(i)).astype(BF16)
            rows = slice(64 * i, 64 * i + 64)
            kss[0, hs, rows, :] = block[0:64, :]
            u1s[hs, 128 * i : 128 * i + 128, :] = block[64:192, :]
            kss[1, hs, rows, :] = block[192:256, :]
            sr[1, hs, rows, :] = dot(xt[hs * 4 + i, 192:256, :], read_e(i)).astype(BF16)

    load_a.wait()
    for q in range(2):
        part = []
        for i in (2 * q, 2 * q + 1):
            weights = yk[2 * i : 2 * i + 2].reshape(256, 256)
            both = dot(a_v[:, 256 * i : 256 * i + 256], weights)
            part.append(both[:, 0:128])
            ame[:, 128 * i : 128 * i + 128] = both[:, 128:256].astype(BF16)
        ams[:, 128 * q : 128 * q + 128] = jnp.where(low1024, part[0], part[1]).astype(BF16)
        amr[:, 128 * q : 128 * q + 128] = jnp.where(low1024, part[1], part[0]).astype(BF16)

    def block_of(ref):
        return lambda i: ref[256 * i : 256 * i + 256, :]

    select_first(block_of(amr), block_of(ame), h)
    send_sr = to_k(sr.at[0, h], spart.at[0, h], 4)
    send_sr.start()

    load_i2.wait()
    send_i2.wait_recv()
    for k in range(8):
        p2v[k] = jnp.concatenate(halves(i2_v[k // 4, k % 4]), axis=0)
    bottoms = []
    for n in order:
        both = dot(p2v[rows2[0, n]], halfs[n])
        bottom = both[0:64, :] + both[64:128, :]
        accv[n + 1] = bottom.astype(BF16)
        bottoms.append(turned(bottom, cols2[0, n], 1 - n // 8))
        if n >= 8:
            vq[n - 8] = jnp.where(low64, bottoms[-2], bottoms[-1]).astype(BF16)
        if n in (11, 15):
            part = pl.ds(n - 11, 4)
            sends_q.append(to_x(vq.at[part], vq_in.at[part], 3 + (n - 11) // 4))
            sends_q[-1].start()

    def link(acc, n, before, value):
        acc[n + 1] = (value + acc[before].astype(F32)).astype(BF16)

    def coupling(acc, table, lanes):
        def read(i):
            blocks = [[acc[table[1, 4 * j + m], :, lanes] for m in range(4)] for j in (2 * i, 2 * i + 1)]
            return jnp.concatenate([jnp.concatenate(row, axis=1) for row in blocks], axis=0)

        return read

    def merged(acc, table, swapped):
        def read(i):
            blocks = []
            for j in (2 * i, 2 * i + 1):
                t = [acc[table[1, 4 * j + m], :, 0:128] for m in range(4)]
                pick = ((1, 0), (3, 2)) if swapped else ((0, 1), (2, 3))
                blocks.append(jnp.concatenate([jnp.where(low128, t[x], t[y]) for x, y in pick], axis=1))
            return jnp.concatenate(blocks, axis=0)

        return read

    load_t1.wait()
    send_i1.wait_recv()
    for i in range(4):
        weighted = fold_inverse(other, i, 4 + i)
        for m in range(2):
            orp[2 * i + m] = weighted[128 * m : 128 * m + 128, :]
    accb[0] = jnp.zeros((128, 128), BF16)
    for n in range(NT):
        link(accb, n, own_s[0, n], dot(t1_v[n], orp[cols1[0, n]]))
    read = coupling(accb, own_s, slice(0, 128))
    for i in range(4):
        spart[0, h, 64 * i : 64 * i + 64, :] = dot(xt[h * 4 + i, 0:64, :], read(i)).astype(BF16)

    send_t1.wait_recv()
    send_tab_k.wait_recv()
    k_tab = pltpu.make_async_copy(tab_k, k_s, loc.at[7])
    k_tab.start()
    k_tab.wait()
    accc[0] = jnp.zeros((128, 256), BF16)
    for n in range(NT):
        link(accc, n, k_s[0, n], dot(t1_in[n], yk[k_s[4, n]]))
    read_e = coupling(accc, k_s, slice(128, 256))
    select_first(merged(accc, k_s, True), read_e, other)

    send_sr.wait_recv()
    sends_l = []
    for hs in range(2):
        own = dot(sr[0, hs], u1r[h])
        far = dot(spart[0, hs], u1r[other])
        lsr[hs] = (ksr[hs].astype(F32) - own - far).astype(BF16)
        sends_l.append(to_k(lsr.at[hs], lsr_in.at[hs], 5 + hs))
        sends_l[-1].start()

    for n in range(NT):
        before = own_s[2, n]
        link(acct, n, before, acct[n + 1].astype(F32))
        link(accv, n, before, accv[n + 1].astype(F32))
    for i in range(8):
        hs, i4 = i // 4, i % 4
        for q in range(2):
            e_at, o_at = own_s[3, 4 * i + 2 * q], own_s[3, 4 * i + 2 * q + 1]
            lanes = slice(128 * q, 128 * q + 128)
            swap = 64 * (i4 ^ 1)
            bss[64 * i : 64 * i + 64, lanes] = jnp.where(low64, acct[e_at], acct[o_at])
            bsr[64 * i : 64 * i + 64, lanes] = jnp.where(low64, acct[o_at], acct[e_at])
            vown[hs, swap : swap + 64, lanes] = jnp.where(low64, accv[e_at], accv[o_at])
    send_bsr = to_k(bsr, bsr_in, 7)
    send_bsr.start()

    select_later(block_of(ams), block_of(ame), h)
    send_sr1 = to_k(sr.at[1, h], spart.at[1, h], 9)
    send_sr1.start()
    for i in range(4):
        spart[1, h, 64 * i : 64 * i + 64, :] = dot(xt[h * 4 + i, 192:256, :], read(i)).astype(BF16)

    sends_p = []
    for hs in range(2):
        sends_l[hs].wait_recv()
        for m in range(2):
            at = 256 * hs + 128 * m
            rows = slice(128 * m, 128 * m + 128)
            total = bss[at : at + 128, :].astype(F32) - dot(lsr[hs, rows, :], vown[h]) - dot(lsr_in[hs, rows, :], vown[other])
            p_out[at : at + 128, :] = total.astype(BF16)
            part = pl.ds(at, 128)
            sends_p.append(to_x(p_out.at[part], p_in.at[part], 5 + 2 * hs + m))
            sends_p[-1].start()

    select_later(merged(accc, k_s, False), read_e, other)
    for hs in range(2):
        own = dot(sr[0, hs], u1s[h])
        far = dot(spart[0, hs], u1s[other])
        lss[hs] = kss[0, hs].astype(F32) - own - far

    send_tab_x.wait_recv()
    x_tab = pltpu.make_async_copy(tab_x, x_s, loc.at[8])
    x_tab.start()
    x_tab.wait()
    for send in sends_q:
        send.wait_recv()
    accxs[0] = jnp.zeros((64, 128), BF16)
    accxv[0] = jnp.zeros((64, 128), BF16)
    for n in range(NT):
        link(accxs, n, x_s[2, n], turned(srq_in[n % 8].astype(F32), x_s[5, n], n // 8))
        link(accxv, n, x_s[2, n], turned(vq_in[n % 8].astype(F32), x_s[5, n], 1 - n // 8))
    for i in range(8):
        hs, i4 = i // 4, i % 4
        for q in range(2):
            e_at, o_at = x_s[3, 4 * i + 2 * q], x_s[3, 4 * i + 2 * q + 1]
            lanes = slice(128 * q, 128 * q + 128)
            swap = 64 * (i4 ^ 1)
            vx[hs, swap : swap + 64, lanes] = jnp.where(low64, accxv[e_at], accxv[o_at])
            csr[64 * i : 64 * i + 64, lanes] = jnp.where(low64, accxs[o_at], accxs[e_at])
    send_csr = to_k(csr, csr_in, 8)
    send_csr.start()

    send_sr1.wait_recv()
    for hs in range(2):
        own = dot(sr[1, hs], u1s[h])
        far = dot(spart[1, hs], u1s[other])
        high, rest = halves(kss[1, hs].astype(F32) - own - far)
        for q in range(2):
            pack = packed(i2_v, hs, q)
            anti = jnp.concatenate([jnp.where(low64, 0.0, pack), jnp.where(low64, pack, 0.0)], axis=0)
            a_high, a_rest = halves(anti)
            rows = slice(128 * q, 128 * q + 128)
            total = dot(a_high, high[rows, :]) + dot(a_rest, high[rows, :]) + dot(a_high, rest[rows, :])
            uu[hs, rows, :] = total.astype(BF16)

    send_bsr.wait_recv()
    top = pl.multiple_of(c * 512, 512)
    bottom = pl.multiple_of(512 - c * 512, 512)
    for hs in range(2):
        rows = slice(256 * hs, 256 * hs + 256)
        total = lss[hs] - dot(lsr[hs], uu[h]) - dot(lsr_in[hs], uu[other])
        total = total - dot(bsr[rows, :], vx[h]) - dot(bsr_in[rows, :], vx[other])
        out_ref[0, pl.ds(top + 256 * hs, 256), :] = total.astype(BF16)
    send_csr.wait_recv()
    for hs in range(2):
        rows = slice(256 * hs, 256 * hs + 256)
        lss[hs] = dot(csr[rows, :], uu[h]) + dot(csr_in[rows, :], uu[other])
    for m in range(4):
        at = 128 * m
        rows = slice(128 * (m % 2), 128 * (m % 2) + 128)
        sends_p[m].wait_recv()
        total = p_in[at : at + 128, :].astype(F32) - lss[m // 2, rows, :]
        out_ref[0, pl.ds(bottom + at, 128), :] = total.astype(BF16)

    for send in (send_t1, send_i1, send_i2, send_tab_k, send_tab_x, send_sr, send_sr1, *sends_q, *sends_l, send_bsr, *sends_p, send_csr):
        send.wait_send()


def local(*args):
    schur, t1, rows1, cols1, count1, o1, i1, t2, rows2, cols2, count2, o2, i2 = args
    hbm = pl.BlockSpec(memory_space=pltpu.HBM)
    label = pltpu.SMEM((1, 16), jnp.int32)
    count = pltpu.SMEM((1,), jnp.int32)
    vmem = pltpu.VMEM
    table = vmem((8, 128), jnp.int32)
    table_s = pltpu.SMEM((8, 128), jnp.int32)
    tiles = vmem((16, 128, 128), BF16)
    panel = vmem((512, 256), BF16)
    panels = vmem((2, 256, 256), BF16)
    onehots = vmem((8, 128, 128), BF16)
    chained = vmem((17, 64, 128), BF16)
    quads = vmem((8, 64, 128), BF16)
    dma = pltpu.SemaphoreType.DMA
    scratch = [
        label, label, count, label, label, count,
        vmem((1024, 1024), BF16), tiles, tiles, tiles,
        vmem((2, 8, 64, 64), F32), vmem((2, 4, 64, 64), F32), vmem((16, 128), jnp.int32), vmem((16, 128), jnp.int32),
        table, table, table, table_s, table_s, table_s,
        vmem((8, 256, 256), BF16), vmem((8, 128, 256), BF16), onehots, onehots, vmem((8, 128, 64), BF16), vmem((4, 128, 128), BF16),
        vmem((17, 128, 128), BF16), vmem((17, 128, 256), BF16), chained, chained, chained, chained, vmem((16, 64, 128), BF16),
        quads, quads, quads, quads,
        vmem((1024, 256), BF16), vmem((1024, 256), BF16), vmem((1024, 512), BF16),
        panels, vmem((2, 2, 256, 256), BF16), vmem((2, 512, 256), BF16), vmem((2, 512, 256), BF16),
        vmem((2, 2, 256, 512), BF16), vmem((2, 2, 256, 512), BF16),
        vmem((2, 256, 256), F32), panels, panels, panels, panels, panels,
        panel, panel, panel, panel, panel, panel, panel,
        dma((16,)), dma((10,)), dma((10,)), dma((9,)), dma((9,)),
    ]
    large = [pltpu.with_memory_space_constraint(x, pltpu.HBM) for x in (schur, t1, t2, i1, i2, o1, o2)]
    return pl.pallas_call(
        kernel,
        out_shape=pltpu.VMEM((1, 1024, 256), BF16),
        in_specs=[hbm] * 13,
        out_specs=pl.BlockSpec(memory_space=pltpu.VMEM),
        scratch_shapes=scratch,
        compiler_params=pltpu.CompilerParams(collective_id=0, has_side_effects=True, vmem_limit_bytes=62 * 2**20),
    )(*large, rows1, cols1, count1, rows2, cols2, count2)


def solution(mesh):
    boxes = ("leaf", "blk")
    return jax.shard_map(
        local,
        mesh=mesh,
        in_specs=(
            P(boxes, None, None),
            P(boxes, None, None, None),
            P(boxes, None),
            P(boxes, None),
            P(boxes),
            P(),
            P(boxes, None, None, None),
            P(boxes, None, None, None),
            P(boxes, None),
            P(boxes, None),
            P(boxes),
            P(),
            P(boxes, None, None, None),
        ),
        out_specs=P(boxes, None, None),
        check_vma=False,
    )
```

```python
import jax
import jax.numpy as jnp
from jax import lax
from jax.experimental import pallas as pl
from jax.experimental.pallas import tpu as pltpu
from jax.sharding import PartitionSpec as P

MESH = pl.DeviceIdType.MESH
F32 = jnp.float32
BF16 = jnp.bfloat16
NT = 16


def dot(a, b):
    return jnp.dot(a, b, preferred_element_type=F32)


def chain_table(rows, cols, count, halved, lane):
    live = count[0]
    targets = [rows[0, n] * 4 + (cols[0, n] >> halved) for n in range(NT)]
    along = jnp.full((1, 128), -1, jnp.int32)
    columns = jnp.zeros((1, 128), jnp.int32)
    for n in range(NT):
        along = jnp.where(lane == n, targets[n], along)
        columns = jnp.where(lane == n, cols[0, n], columns)
    prev = jnp.zeros((1, 128), jnp.int32)
    last = jnp.zeros((1, 128), jnp.int32)
    for n in range(NT):
        value = jnp.where(n < live, n + 1, 0)
        prev = jnp.maximum(prev, jnp.where((along == targets[n]) & (lane > n), value, 0))
        last = jnp.maximum(last, jnp.where(lane == targets[n], value, 0))
    return prev, last, columns


def halves(value):
    high = value.astype(BF16)
    return high, (value - high.astype(F32)).astype(BF16)


def kernel(
    a_hbm, t1_hbm, t2_hbm, i1_hbm, i2_hbm, o1_hbm, o2_hbm,
    rows1_hbm, cols1_hbm, count1_hbm, rows2_hbm, cols2_hbm, count2_hbm,
    out_ref,
    rows1, cols1, count1, rows2, cols2, count2,
    a_v, t1_v, t1_in, t2_v, i1_v, i2_v, o1_v, o2_v,
    tab, tab_k, tab_x, own_s, k_s, x_s,
    pack1, xt, yk, orp, p2s, p2v, p2x,
    accb, accc, acct, accv, accxs, accxv, halfs, srq, srq_in, vq, vq_in,
    ams, amr, ame, ksr, kss, u1r, u1s, sr, spart,
    lss, lsr, lsr_in, uu, vown, vx,
    bss, bsr, bsr_in, csr, csr_in, p_out, p_in,
    loc, ksend, krecv, xsend, xrecv,
):
    leaf = lax.axis_index("leaf")
    c = lax.axis_index("blk")
    r = leaf // 2
    h = leaf - 2 * r
    other = 1 - h
    kid = {"leaf": leaf + 1 - 2 * h}
    xid = {"blk": 1 - c}

    def to_k(src, dst, n):
        return pltpu.make_async_remote_copy(
            src_ref=src, dst_ref=dst, send_sem=ksend.at[n], recv_sem=krecv.at[n],
            device_id=kid, device_id_type=MESH,
        )

    def to_x(src, dst, n):
        return pltpu.make_async_remote_copy(
            src_ref=src, dst_ref=dst, send_sem=xsend.at[n], recv_sem=xrecv.at[n],
            device_id=xid, device_id_type=MESH,
        )

    barrier = pltpu.get_barrier_semaphore()
    pl.semaphore_signal(barrier, inc=1, device_id=xid, device_id_type=MESH)
    pl.semaphore_signal(barrier, inc=1, device_id=kid, device_id_type=MESH)

    pairs = (
        (rows2_hbm, rows2), (cols2_hbm, cols2), (count2_hbm, count2),
        (rows1_hbm, rows1), (cols1_hbm, cols1), (count1_hbm, count1),
    )
    load_labels = [pltpu.make_async_copy(src, dst, loc.at[9 + n]) for n, (src, dst) in enumerate(pairs)]
    load_o1 = pltpu.make_async_copy(o1_hbm.at[2 * r + c], o1_v, loc.at[0])
    load_o2 = pltpu.make_async_copy(o2_hbm.at[r], o2_v, loc.at[1])
    load_t2 = pltpu.make_async_copy(t2_hbm.at[0], t2_v, loc.at[2])
    load_i2 = pltpu.make_async_copy(i2_hbm.at[0], i2_v.at[h], loc.at[3])
    load_i1 = pltpu.make_async_copy(i1_hbm.at[0], i1_v, loc.at[4])
    load_a = pltpu.make_async_copy(a_hbm.at[0], a_v, loc.at[5])
    load_t1 = pltpu.make_async_copy(t1_hbm.at[0], t1_v, loc.at[15])
    for load in (load_o2, *load_labels, load_t2, load_o1, load_i1, load_a, load_i2, load_t1):
        load.start()

    wide = lax.broadcasted_iota(jnp.int32, (128, 256), 1).astype(BF16)
    tall = lax.broadcasted_iota(jnp.int32, (256, 128), 0).astype(BF16)
    square = tall[0:128, :]
    low8 = lax.broadcasted_iota(jnp.int32, (8, 128), 1) < 64
    low64 = lax.broadcasted_iota(jnp.int32, (64, 128), 1) < 64
    low1024 = lax.broadcasted_iota(jnp.int32, (1024, 128), 1) < 64
    low128 = lax.broadcasted_iota(jnp.int32, (128, 128), 1) < 64
    lane = lax.broadcasted_iota(jnp.int32, (1, 128), 1)

    one, zero = jnp.asarray(1, BF16), jnp.asarray(0, BF16)

    def onehot(rows, index):
        return jnp.where(rows == index.astype(BF16), one, zero)

    load_o2.wait()
    base = pl.multiple_of(c * 8, 8)
    mine2 = o2_v[pl.ds(base, 8), :]
    theirs2 = o2_v[pl.ds(pl.multiple_of(8 - base, 8), 8), :]
    theirs2 = jnp.where(h == 0, theirs2, pltpu.roll(theirs2, 4, 0))
    columns2 = mine2.astype(F32).T
    for i in range(4):
        row = theirs2[i : i + 1, :]
        p2x[i] = onehot(square, pltpu.roll(row, 64, 1) if i % 2 else row)
    for k in range(8):
        p2s[k] = onehot(wide[:, 0:128], columns2[:, k : k + 1])

    def turned(value, column, wanted):
        return jnp.where((column & 1) == wanted, pltpu.roll(value, 64, 1), value)

    load_i1.wait()
    for i in range(4):
        pack1[h, i] = jnp.concatenate([i1_v[2 * i], i1_v[2 * i + 1]], axis=1).astype(BF16)
    for load in load_labels[:2]:
        load.wait()
    load_t2.wait()
    acct[0] = jnp.zeros((64, 128), BF16)
    accv[0] = jnp.zeros((64, 128), BF16)
    sends_q = []
    tops = []
    order = [n for m in range(8) for n in (m, m + 8)]
    for n in order:
        half = dot(t2_v[n], p2x[cols2[0, n]]).astype(BF16)
        both = dot(p2s[rows2[0, n]], half)
        top = both[0:64, :]
        halfs[n] = both[64:128, :].astype(BF16)
        acct[n + 1] = top.astype(BF16)
        tops.append(turned(top, cols2[0, n], n // 8))
        if n >= 8:
            srq[n - 8] = jnp.where(low64, tops[-2], tops[-1]).astype(BF16)

    pl.semaphore_wait(barrier, 2)
    send_t1 = to_k(t1_hbm.at[0], t1_in, 0)
    send_i1 = to_k(pack1.at[h], pack1.at[h], 1)
    send_i2 = to_k(i2_hbm.at[0], i2_v.at[h], 2)
    for send in (send_i2, send_i1, send_t1):
        send.start()
    sends_q.append(to_x(srq, srq_in, 1))
    sends_q[-1].start()

    for load in load_labels[2:]:
        load.wait()
    prev1, last1, cols_row1 = chain_table(rows1, cols1, count1, 1, lane)
    prev2, last2, cols_row2 = chain_table(rows2, cols2, count2, 0, lane)
    tab[0:1, :] = prev1
    tab[1:2, :] = last1
    tab[2:3, :] = prev2
    tab[3:4, :] = last2
    tab[4:5, :] = cols_row1
    tab[5:6, :] = cols_row2
    tab[6:8, :] = jnp.zeros((2, 128), jnp.int32)
    own_tab = pltpu.make_async_copy(tab, own_s, loc.at[6])
    own_tab.start()
    send_tab_k = to_k(tab, tab_k, 3)
    send_tab_k.start()
    send_tab_x = to_x(tab, tab_x, 0)
    send_tab_x.start()

    load_o1.wait()
    even = o1_v[pl.ds(0, 8, stride=2), :]
    odd = o1_v[pl.ds(1, 8, stride=2), :]
    shift = jnp.where(low8, 0, 128)
    skel = jnp.where(low8, even, pltpu.roll(odd, 64, 1)) + shift
    redu = jnp.where(low8, pltpu.roll(even, 64, 1), odd) + shift
    comp = jnp.take_along_axis(skel, mine2, axis=1, mode="promise_in_bounds")
    columns = jnp.concatenate([comp, redu], axis=0).astype(F32).T
    comp_own = jnp.where(h == 0, comp, pltpu.roll(comp, 4, 0))
    redu_own = jnp.where(h == 0, redu, pltpu.roll(redu, 4, 0))
    for k in range(8):
        xt[k, 0:64, :] = onehot(wide[0:64, :], columns[0:64, k : k + 1])
        xt[k, 192:256, :] = onehot(wide[64:128, :], columns[64:128, k : k + 1])
        xt[k, 64:128, 0:128] = onehot(wide[0:64, 0:128], columns[0:64, 8 + k : 9 + k])
        xt[k, 64:128, 128:256] = jnp.zeros((64, 128), BF16)
        xt[k, 128:192, 0:128] = jnp.zeros((64, 128), BF16)
        xt[k, 128:192, 128:256] = onehot(wide[0:64, 128:256], columns[64:128, 8 + k : 9 + k])

    def packed(ref, hs, q):
        return jnp.concatenate([ref[hs, 2 * q], ref[hs, 2 * q + 1]], axis=1)

    def fold_inverse(hs, i, index):
        pack = pack1[hs, i]
        diag = jnp.concatenate([jnp.where(low64, pack, zero), jnp.where(low64, zero, pack)], axis=0)
        return dot(onehot(tall, redu_own[index : index + 1, :]), diag).astype(BF16)

    for i in range(4):
        row = comp_own[i : i + 1, :]
        skeleton = onehot(tall, pltpu.roll(row, 64, 1) if i % 2 else row)
        weighted = fold_inverse(h, i, i)
        for m in range(2):
            yk[2 * i + m, :, 0:128] = skeleton[128 * m : 128 * m + 128, :]
            yk[2 * i + m, :, 128:256] = weighted[128 * m : 128 * m + 128, :]

    def select_first(read_r, read_e, hs):
        for i in range(4):
            block = dot(xt[hs * 4 + i, 0:192, :], read_r(i)).astype(BF16)
            rows = slice(64 * i, 64 * i + 64)
            ksr[hs, rows, :] = block[0:64, :]
            u1r[hs, 128 * i : 128 * i + 128, :] = block[64:192, :]
            sr[0, hs, rows, :] = dot(xt[hs * 4 + i, 0:64, :], read_e(i)).astype(BF16)

    def select_later(read_s, read_e, hs):
        for i in range(4):
            block = dot(xt[hs * 4 + i], read_s(i)).astype(BF16)
            rows = slice(64 * i, 64 * i + 64)
            kss[0, hs, rows, :] = block[0:64, :]
            u1s[hs, 128 * i : 128 * i + 128, :] = block[64:192, :]
            kss[1, hs, rows, :] = block[192:256, :]
            sr[1, hs, rows, :] = dot(xt[hs * 4 + i, 192:256, :], read_e(i)).astype(BF16)

    load_a.wait()
    for q in range(2):
        part = []
        for i in (2 * q, 2 * q + 1):
            weights = yk[2 * i : 2 * i + 2].reshape(256, 256)
            both = dot(a_v[:, 256 * i : 256 * i + 256], weights)
            part.append(both[:, 0:128])
            ame[:, 128 * i : 128 * i + 128] = both[:, 128:256].astype(BF16)
        ams[:, 128 * q : 128 * q + 128] = jnp.where(low1024, part[0], part[1]).astype(BF16)
        amr[:, 128 * q : 128 * q + 128] = jnp.where(low1024, part[1], part[0]).astype(BF16)

    def block_of(ref):
        return lambda i: ref[256 * i : 256 * i + 256, :]

    select_first(block_of(amr), block_of(ame), h)
    send_sr = to_k(sr.at[0, h], spart.at[0, h], 4)
    send_sr.start()

    load_i2.wait()
    send_i2.wait_recv()
    for k in range(8):
        p2v[k] = jnp.concatenate(halves(i2_v[k // 4, k % 4]), axis=0)
    bottoms = []
    for n in order:
        both = dot(p2v[rows2[0, n]], halfs[n])
        bottom = both[0:64, :] + both[64:128, :]
        accv[n + 1] = bottom.astype(BF16)
        bottoms.append(turned(bottom, cols2[0, n], 1 - n // 8))
        if n >= 8:
            vq[n - 8] = jnp.where(low64, bottoms[-2], bottoms[-1]).astype(BF16)
        if n in (11, 15):
            part = pl.ds(n - 11, 4)
            sends_q.append(to_x(vq.at[part], vq_in.at[part], 2 + (n - 11) // 4))
            sends_q[-1].start()

    def link(acc, n, before, value):
        acc[n + 1] = (value + acc[before].astype(F32)).astype(BF16)

    def coupling(acc, table, lanes):
        def read(i):
            blocks = [[acc[table[1, 4 * j + m], :, lanes] for m in range(4)] for j in (2 * i, 2 * i + 1)]
            return jnp.concatenate([jnp.concatenate(row, axis=1) for row in blocks], axis=0)

        return read

    def merged(acc, table, swapped):
        def read(i):
            blocks = []
            for j in (2 * i, 2 * i + 1):
                t = [acc[table[1, 4 * j + m], :, 0:128] for m in range(4)]
                pick = ((1, 0), (3, 2)) if swapped else ((0, 1), (2, 3))
                blocks.append(jnp.concatenate([jnp.where(low128, t[x], t[y]) for x, y in pick], axis=1))
            return jnp.concatenate(blocks, axis=0)

        return read

    own_tab.wait()
    send_tab_k.wait_recv()
    k_tab = pltpu.make_async_copy(tab_k, k_s, loc.at[7])
    k_tab.start()
    load_t1.wait()
    send_i1.wait_recv()
    for i in range(4):
        weighted = fold_inverse(other, i, 4 + i)
        for m in range(2):
            orp[2 * i + m] = weighted[128 * m : 128 * m + 128, :]
    accb[0] = jnp.zeros((128, 128), BF16)
    for n in range(NT):
        link(accb, n, own_s[0, n], dot(t1_v[n], orp[cols1[0, n]]))
    read = coupling(accb, own_s, slice(0, 128))
    for i in range(4):
        spart[0, h, 64 * i : 64 * i + 64, :] = dot(xt[h * 4 + i, 0:64, :], read(i)).astype(BF16)

    send_t1.wait_recv()
    k_tab.wait()
    accc[0] = jnp.zeros((128, 256), BF16)
    for n in range(NT):
        link(accc, n, k_s[0, n], dot(t1_in[n], yk[k_s[4, n]]))
    read_e = coupling(accc, k_s, slice(128, 256))
    select_first(merged(accc, k_s, True), read_e, other)

    send_sr.wait_recv()
    sends_l = []
    for hs in range(2):
        own = dot(sr[0, hs], u1r[h])
        far = dot(spart[0, hs], u1r[other])
        lsr[hs] = (ksr[hs].astype(F32) - own - far).astype(BF16)
        sends_l.append(to_k(lsr.at[hs], lsr_in.at[hs], 5 + hs))
        sends_l[-1].start()

    for n in range(NT):
        before = own_s[2, n]
        link(acct, n, before, acct[n + 1].astype(F32))
        link(accv, n, before, accv[n + 1].astype(F32))
    for i in range(8):
        hs, i4 = i // 4, i % 4
        for q in range(2):
            e_at, o_at = own_s[3, 4 * i + 2 * q], own_s[3, 4 * i + 2 * q + 1]
            lanes = slice(128 * q, 128 * q + 128)
            swap = 64 * (i4 ^ 1)
            bss[64 * i : 64 * i + 64, lanes] = jnp.where(low64, acct[e_at], acct[o_at])
            bsr[64 * i : 64 * i + 64, lanes] = jnp.where(low64, acct[o_at], acct[e_at])
            vown[hs, swap : swap + 64, lanes] = jnp.where(low64, accv[e_at], accv[o_at])
    send_bsr = to_k(bsr, bsr_in, 7)
    send_bsr.start()

    send_tab_x.wait_recv()
    x_tab = pltpu.make_async_copy(tab_x, x_s, loc.at[8])
    x_tab.start()
    select_later(block_of(ams), block_of(ame), h)
    send_sr1 = to_k(sr.at[1, h], spart.at[1, h], 9)
    send_sr1.start()
    for i in range(4):
        spart[1, h, 64 * i : 64 * i + 64, :] = dot(xt[h * 4 + i, 192:256, :], read(i)).astype(BF16)

    sends_p = []
    for hs in range(2):
        sends_l[hs].wait_recv()
        for m in range(2):
            at = 256 * hs + 128 * m
            rows = slice(128 * m, 128 * m + 128)
            total = bss[at : at + 128, :].astype(F32) - dot(lsr[hs, rows, :], vown[h]) - dot(lsr_in[hs, rows, :], vown[other])
            p_out[at : at + 128, :] = total.astype(BF16)
            part = pl.ds(at, 128)
            sends_p.append(to_x(p_out.at[part], p_in.at[part], 4 + 2 * hs + m))
            sends_p[-1].start()

    select_later(merged(accc, k_s, False), read_e, other)
    for hs in range(2):
        own = dot(sr[0, hs], u1s[h])
        far = dot(spart[0, hs], u1s[other])
        lss[hs] = kss[0, hs].astype(F32) - own - far

    x_tab.wait()
    for send in sends_q:
        send.wait_recv()
    accxs[0] = jnp.zeros((64, 128), BF16)
    accxv[0] = jnp.zeros((64, 128), BF16)
    for n in range(NT):
        link(accxs, n, x_s[2, n], turned(srq_in[n % 8].astype(F32), x_s[5, n], n // 8))
        link(accxv, n, x_s[2, n], turned(vq_in[n % 8].astype(F32), x_s[5, n], 1 - n // 8))
    for i in range(8):
        hs, i4 = i // 4, i % 4
        for q in range(2):
            e_at, o_at = x_s[3, 4 * i + 2 * q], x_s[3, 4 * i + 2 * q + 1]
            lanes = slice(128 * q, 128 * q + 128)
            swap = 64 * (i4 ^ 1)
            vx[hs, swap : swap + 64, lanes] = jnp.where(low64, accxv[e_at], accxv[o_at])
            csr[64 * i : 64 * i + 64, lanes] = jnp.where(low64, accxs[o_at], accxs[e_at])
    send_csr = to_k(csr, csr_in, 8)
    send_csr.start()

    send_sr1.wait_recv()
    for hs in range(2):
        own = dot(sr[1, hs], u1s[h])
        far = dot(spart[1, hs], u1s[other])
        high, rest = halves(kss[1, hs].astype(F32) - own - far)
        for q in range(2):
            pack = packed(i2_v, hs, q)
            anti = jnp.concatenate([jnp.where(low64, 0.0, pack), jnp.where(low64, pack, 0.0)], axis=0)
            a_high, a_rest = halves(anti)
            rows = slice(128 * q, 128 * q + 128)
            total = dot(a_high, high[rows, :]) + dot(a_rest, high[rows, :]) + dot(a_high, rest[rows, :])
            uu[hs, rows, :] = total.astype(BF16)

    send_bsr.wait_recv()
    top = pl.multiple_of(c * 512, 512)
    bottom = pl.multiple_of(512 - c * 512, 512)
    for hs in range(2):
        rows = slice(256 * hs, 256 * hs + 256)
        total = lss[hs] - dot(lsr[hs], uu[h]) - dot(lsr_in[hs], uu[other])
        total = total - dot(bsr[rows, :], vx[h]) - dot(bsr_in[rows, :], vx[other])
        out_ref[0, pl.ds(top + 256 * hs, 256), :] = total.astype(BF16)
    send_csr.wait_recv()
    for hs in range(2):
        rows = slice(256 * hs, 256 * hs + 256)
        lss[hs] = dot(csr[rows, :], uu[h]) + dot(csr_in[rows, :], uu[other])
    for m in range(4):
        at = 128 * m
        rows = slice(128 * (m % 2), 128 * (m % 2) + 128)
        sends_p[m].wait_recv()
        total = p_in[at : at + 128, :].astype(F32) - lss[m // 2, rows, :]
        out_ref[0, pl.ds(bottom + at, 128), :] = total.astype(BF16)

    for send in (send_t1, send_i1, send_i2, send_tab_k, send_tab_x, send_sr, send_sr1, *sends_q, *sends_l, send_bsr, *sends_p, send_csr):
        send.wait_send()


def local(*args):
    schur, t1, rows1, cols1, count1, o1, i1, t2, rows2, cols2, count2, o2, i2 = args
    hbm = pl.BlockSpec(memory_space=pltpu.HBM)
    label = pltpu.SMEM((1, 16), jnp.int32)
    count = pltpu.SMEM((1,), jnp.int32)
    vmem = pltpu.VMEM
    table = vmem((8, 128), jnp.int32)
    table_s = pltpu.SMEM((8, 128), jnp.int32)
    tiles = vmem((16, 128, 128), BF16)
    panel = vmem((512, 256), BF16)
    panels = vmem((2, 256, 256), BF16)
    onehots = vmem((8, 128, 128), BF16)
    chained = vmem((17, 64, 128), BF16)
    quads = vmem((8, 64, 128), BF16)
    dma = pltpu.SemaphoreType.DMA
    scratch = [
        label, label, count, label, label, count,
        vmem((1024, 1024), BF16), tiles, tiles, tiles,
        vmem((8, 64, 64), F32), vmem((2, 4, 64, 64), F32), vmem((16, 128), jnp.int32), vmem((16, 128), jnp.int32),
        table, table, table, table_s, table_s, table_s,
        vmem((2, 4, 64, 128), BF16), vmem((8, 256, 256), BF16), vmem((8, 128, 256), BF16), onehots, onehots, vmem((8, 128, 64), BF16), vmem((4, 128, 128), BF16),
        vmem((17, 128, 128), BF16), vmem((17, 128, 256), BF16), chained, chained, chained, chained, vmem((16, 64, 128), BF16),
        quads, quads, quads, quads,
        vmem((1024, 256), BF16), vmem((1024, 256), BF16), vmem((1024, 512), BF16),
        panels, vmem((2, 2, 256, 256), BF16), vmem((2, 512, 256), BF16), vmem((2, 512, 256), BF16),
        vmem((2, 2, 256, 512), BF16), vmem((2, 2, 256, 512), BF16),
        vmem((2, 256, 256), F32), panels, panels, panels, panels, panels,
        panel, panel, panel, panel, panel, panel, panel,
        dma((16,)), dma((10,)), dma((10,)), dma((8,)), dma((8,)),
    ]
    large = [pltpu.with_memory_space_constraint(x, pltpu.HBM) for x in (schur, t1, t2, i1, i2, o1, o2)]
    return pl.pallas_call(
        kernel,
        out_shape=pltpu.VMEM((1, 1024, 256), BF16),
        in_specs=[hbm] * 13,
        out_specs=pl.BlockSpec(memory_space=pltpu.VMEM),
        scratch_shapes=scratch,
        compiler_params=pltpu.CompilerParams(collective_id=0, has_side_effects=True, vmem_limit_bytes=62 * 2**20),
    )(*large, rows1, cols1, count1, rows2, cols2, count2)


def solution(mesh):
    boxes = ("leaf", "blk")
    return jax.shard_map(
        local,
        mesh=mesh,
        in_specs=(
            P(boxes, None, None),
            P(boxes, None, None, None),
            P(boxes, None),
            P(boxes, None),
            P(boxes),
            P(),
            P(boxes, None, None, None),
            P(boxes, None, None, None),
            P(boxes, None),
            P(boxes, None),
            P(boxes),
            P(),
            P(boxes, None, None, None),
        ),
        out_specs=P(boxes, None, None),
        check_vma=False,
    )
```

```python
import jax
import jax.numpy as jnp
from jax import lax
from jax.experimental import pallas as pl
from jax.experimental.pallas import tpu as pltpu
from jax.sharding import PartitionSpec as P

MESH = pl.DeviceIdType.MESH
F32 = jnp.float32
BF16 = jnp.bfloat16
NT = 16


def dot(a, b):
    return jnp.dot(a, b, preferred_element_type=F32)


def chain_table(rows, cols, count, halved, lane):
    live = count[0]
    targets = [rows[0, n] * 4 + (cols[0, n] >> halved) for n in range(NT)]
    along = jnp.full((1, 128), -1, jnp.int32)
    columns = jnp.zeros((1, 128), jnp.int32)
    for n in range(NT):
        along = jnp.where(lane == n, targets[n], along)
        columns = jnp.where(lane == n, cols[0, n], columns)
    prev = jnp.zeros((1, 128), jnp.int32)
    last = jnp.zeros((1, 128), jnp.int32)
    for n in range(NT):
        value = jnp.where(n < live, n + 1, 0)
        prev = jnp.maximum(prev, jnp.where((along == targets[n]) & (lane > n), value, 0))
        last = jnp.maximum(last, jnp.where(lane == targets[n], value, 0))
    return prev, last, columns


def halves(value):
    high = value.astype(BF16)
    return high, (value - high.astype(F32)).astype(BF16)


def kernel(
    a_hbm, t1_hbm, t2_hbm, i1_hbm, i2_hbm, o1_hbm, o2_hbm,
    rows1_hbm, cols1_hbm, count1_hbm, rows2_hbm, cols2_hbm, count2_hbm,
    out_ref,
    rows1, cols1, count1, rows2, cols2, count2,
    a_v, t1_v, t1_in, t2_v, i1_v, i2_v, o1_v, o2_v,
    tab, tab_k, tab_x, own_s, k_s, x_s,
    pack1, xt, yk, orp, p2s, p2v, p2x,
    accb, accc, acct, accv, accxs, accxv, halfs, srq, srq_in, vq, vq_in,
    ams, amr, ame, ksr, kss, u1r, u1s, sr, spart,
    lss, lsr, lsr_in, uu, vown, vx,
    bss, bsr, bsr_in, csr, csr_in, p_out, p_in,
    loc, ksend, krecv, xsend, xrecv,
):
    leaf = lax.axis_index("leaf")
    c = lax.axis_index("blk")
    r = leaf // 2
    h = leaf - 2 * r
    other = 1 - h
    kid = {"leaf": leaf + 1 - 2 * h}
    xid = {"blk": 1 - c}

    def to_k(src, dst, n):
        return pltpu.make_async_remote_copy(
            src_ref=src, dst_ref=dst, send_sem=ksend.at[n], recv_sem=krecv.at[n],
            device_id=kid, device_id_type=MESH,
        )

    def to_x(src, dst, n):
        return pltpu.make_async_remote_copy(
            src_ref=src, dst_ref=dst, send_sem=xsend.at[n], recv_sem=xrecv.at[n],
            device_id=xid, device_id_type=MESH,
        )

    barrier = pltpu.get_barrier_semaphore()
    pl.semaphore_signal(barrier, inc=1, device_id=xid, device_id_type=MESH)
    pl.semaphore_signal(barrier, inc=1, device_id=kid, device_id_type=MESH)

    pairs = (
        (rows2_hbm, rows2), (cols2_hbm, cols2), (count2_hbm, count2),
        (rows1_hbm, rows1), (cols1_hbm, cols1), (count1_hbm, count1),
    )
    load_labels = [pltpu.make_async_copy(src, dst, loc.at[9 + n]) for n, (src, dst) in enumerate(pairs)]
    load_o1 = pltpu.make_async_copy(o1_hbm.at[2 * r + c], o1_v, loc.at[0])
    load_o2 = pltpu.make_async_copy(o2_hbm.at[r], o2_v, loc.at[1])
    load_t2 = pltpu.make_async_copy(t2_hbm.at[0], t2_v, loc.at[2])
    load_i2 = pltpu.make_async_copy(i2_hbm.at[0], i2_v.at[h], loc.at[3])
    load_i1 = pltpu.make_async_copy(i1_hbm.at[0], i1_v, loc.at[4])
    load_a = pltpu.make_async_copy(a_hbm.at[0], a_v, loc.at[5])
    load_t1 = pltpu.make_async_copy(t1_hbm.at[0], t1_v, loc.at[15])
    for load in (load_o2, *load_labels, load_t2, load_o1, load_i1, load_a, load_i2, load_t1):
        load.start()

    wide = lax.broadcasted_iota(jnp.int32, (128, 256), 1).astype(BF16)
    tall = lax.broadcasted_iota(jnp.int32, (256, 128), 0).astype(BF16)
    square = tall[0:128, :]
    low8 = lax.broadcasted_iota(jnp.int32, (8, 128), 1) < 64
    low64 = lax.broadcasted_iota(jnp.int32, (64, 128), 1) < 64
    low1024 = lax.broadcasted_iota(jnp.int32, (1024, 128), 1) < 64
    low128 = lax.broadcasted_iota(jnp.int32, (128, 128), 1) < 64
    lane = lax.broadcasted_iota(jnp.int32, (1, 128), 1)

    one, zero = jnp.asarray(1, BF16), jnp.asarray(0, BF16)

    def onehot(rows, index):
        return jnp.where(rows == index.astype(BF16), one, zero)

    load_o2.wait()
    base = pl.multiple_of(c * 8, 8)
    mine2 = o2_v[pl.ds(base, 8), :]
    theirs2 = o2_v[pl.ds(pl.multiple_of(8 - base, 8), 8), :]
    theirs2 = jnp.where(h == 0, theirs2, pltpu.roll(theirs2, 4, 0))
    columns2 = mine2.astype(F32).T
    for i in range(4):
        row = theirs2[i : i + 1, :]
        p2x[i] = onehot(square, pltpu.roll(row, 64, 1) if i % 2 else row)
    for k in range(8):
        p2s[k] = onehot(wide[:, 0:128], columns2[:, k : k + 1])

    def turned(value, column, wanted):
        return jnp.where((column & 1) == wanted, pltpu.roll(value, 64, 1), value)

    load_i1.wait()
    for i in range(4):
        pack1[h, i] = jnp.concatenate([i1_v[2 * i], i1_v[2 * i + 1]], axis=1).astype(BF16)
    for load in load_labels[:2]:
        load.wait()
    load_t2.wait()
    acct[0] = jnp.zeros((64, 128), BF16)
    accv[0] = jnp.zeros((64, 128), BF16)
    sends_q = []
    tops = []
    order = [n for m in range(8) for n in (m, m + 8)]
    for n in order:
        half = dot(t2_v[n], p2x[cols2[0, n]]).astype(BF16)
        both = dot(p2s[rows2[0, n]], half)
        top = both[0:64, :]
        halfs[n] = both[64:128, :].astype(BF16)
        acct[n + 1] = top.astype(BF16)
        tops.append(turned(top, cols2[0, n], n // 8))
        if n >= 8:
            srq[n - 8] = jnp.where(low64, tops[-2], tops[-1]).astype(BF16)

    pl.semaphore_wait(barrier, 2)
    load_i2.wait()
    load_t1.wait()
    send_t1 = to_k(t1_v, t1_in, 0)
    send_i1 = to_k(pack1.at[h], pack1.at[h], 1)
    send_i2 = to_k(i2_v.at[h], i2_v.at[h], 2)
    for send in (send_i2, send_i1, send_t1):
        send.start()
    sends_q.append(to_x(srq, srq_in, 1))
    sends_q[-1].start()

    for load in load_labels[2:]:
        load.wait()
    prev1, last1, cols_row1 = chain_table(rows1, cols1, count1, 1, lane)
    prev2, last2, cols_row2 = chain_table(rows2, cols2, count2, 0, lane)
    tab[0:1, :] = prev1
    tab[1:2, :] = last1
    tab[2:3, :] = prev2
    tab[3:4, :] = last2
    tab[4:5, :] = cols_row1
    tab[5:6, :] = cols_row2
    tab[6:8, :] = jnp.zeros((2, 128), jnp.int32)
    own_tab = pltpu.make_async_copy(tab, own_s, loc.at[6])
    own_tab.start()
    send_tab_k = to_k(tab, tab_k, 3)
    send_tab_k.start()
    send_tab_x = to_x(tab, tab_x, 0)
    send_tab_x.start()

    load_o1.wait()
    even = o1_v[pl.ds(0, 8, stride=2), :]
    odd = o1_v[pl.ds(1, 8, stride=2), :]
    shift = jnp.where(low8, 0, 128)
    skel = jnp.where(low8, even, pltpu.roll(odd, 64, 1)) + shift
    redu = jnp.where(low8, pltpu.roll(even, 64, 1), odd) + shift
    comp = jnp.take_along_axis(skel, mine2, axis=1, mode="promise_in_bounds")
    columns = jnp.concatenate([comp, redu], axis=0).astype(F32).T
    comp_own = jnp.where(h == 0, comp, pltpu.roll(comp, 4, 0))
    redu_own = jnp.where(h == 0, redu, pltpu.roll(redu, 4, 0))
    for k in range(8):
        xt[k, 0:64, :] = onehot(wide[0:64, :], columns[0:64, k : k + 1])
        xt[k, 192:256, :] = onehot(wide[64:128, :], columns[64:128, k : k + 1])
        xt[k, 64:128, 0:128] = onehot(wide[0:64, 0:128], columns[0:64, 8 + k : 9 + k])
        xt[k, 64:128, 128:256] = jnp.zeros((64, 128), BF16)
        xt[k, 128:192, 0:128] = jnp.zeros((64, 128), BF16)
        xt[k, 128:192, 128:256] = onehot(wide[0:64, 128:256], columns[64:128, 8 + k : 9 + k])

    def packed(ref, hs, q):
        return jnp.concatenate([ref[hs, 2 * q], ref[hs, 2 * q + 1]], axis=1)

    def fold_inverse(hs, i, index):
        pack = pack1[hs, i]
        diag = jnp.concatenate([jnp.where(low64, pack, zero), jnp.where(low64, zero, pack)], axis=0)
        return dot(onehot(tall, redu_own[index : index + 1, :]), diag).astype(BF16)

    for i in range(4):
        row = comp_own[i : i + 1, :]
        skeleton = onehot(tall, pltpu.roll(row, 64, 1) if i % 2 else row)
        weighted = fold_inverse(h, i, i)
        for m in range(2):
            yk[2 * i + m, :, 0:128] = skeleton[128 * m : 128 * m + 128, :]
            yk[2 * i + m, :, 128:256] = weighted[128 * m : 128 * m + 128, :]

    def select_first(read_r, read_e, hs):
        for i in range(4):
            block = dot(xt[hs * 4 + i, 0:192, :], read_r(i)).astype(BF16)
            rows = slice(64 * i, 64 * i + 64)
            ksr[hs, rows, :] = block[0:64, :]
            u1r[hs, 128 * i : 128 * i + 128, :] = block[64:192, :]
            sr[0, hs, rows, :] = dot(xt[hs * 4 + i, 0:64, :], read_e(i)).astype(BF16)

    def select_later(read_s, read_e, hs):
        for i in range(4):
            block = dot(xt[hs * 4 + i], read_s(i)).astype(BF16)
            rows = slice(64 * i, 64 * i + 64)
            kss[0, hs, rows, :] = block[0:64, :]
            u1s[hs, 128 * i : 128 * i + 128, :] = block[64:192, :]
            kss[1, hs, rows, :] = block[192:256, :]
            sr[1, hs, rows, :] = dot(xt[hs * 4 + i, 192:256, :], read_e(i)).astype(BF16)

    load_a.wait()
    for q in range(2):
        part = []
        for i in (2 * q, 2 * q + 1):
            weights = yk[2 * i : 2 * i + 2].reshape(256, 256)
            both = dot(a_v[:, 256 * i : 256 * i + 256], weights)
            part.append(both[:, 0:128])
            ame[:, 128 * i : 128 * i + 128] = both[:, 128:256].astype(BF16)
        ams[:, 128 * q : 128 * q + 128] = jnp.where(low1024, part[0], part[1]).astype(BF16)
        amr[:, 128 * q : 128 * q + 128] = jnp.where(low1024, part[1], part[0]).astype(BF16)

    def block_of(ref):
        return lambda i: ref[256 * i : 256 * i + 256, :]

    select_first(block_of(amr), block_of(ame), h)
    send_sr = to_k(sr.at[0, h], spart.at[0, h], 4)
    send_sr.start()

    send_i2.wait_recv()
    for k in range(8):
        p2v[k] = jnp.concatenate(halves(i2_v[k // 4, k % 4]), axis=0)
    bottoms = []
    for n in order:
        both = dot(p2v[rows2[0, n]], halfs[n])
        bottom = both[0:64, :] + both[64:128, :]
        accv[n + 1] = bottom.astype(BF16)
        bottoms.append(turned(bottom, cols2[0, n], 1 - n // 8))
        if n >= 8:
            vq[n - 8] = jnp.where(low64, bottoms[-2], bottoms[-1]).astype(BF16)
        if n in (11, 15):
            part = pl.ds(n - 11, 4)
            sends_q.append(to_x(vq.at[part], vq_in.at[part], 2 + (n - 11) // 4))
            sends_q[-1].start()

    def link(acc, n, before, value):
        acc[n + 1] = (value + acc[before].astype(F32)).astype(BF16)

    def coupling(acc, table, lanes):
        def read(i):
            blocks = [[acc[table[1, 4 * j + m], :, lanes] for m in range(4)] for j in (2 * i, 2 * i + 1)]
            return jnp.concatenate([jnp.concatenate(row, axis=1) for row in blocks], axis=0)

        return read

    def merged(acc, table, swapped):
        def read(i):
            blocks = []
            for j in (2 * i, 2 * i + 1):
                t = [acc[table[1, 4 * j + m], :, 0:128] for m in range(4)]
                pick = ((1, 0), (3, 2)) if swapped else ((0, 1), (2, 3))
                blocks.append(jnp.concatenate([jnp.where(low128, t[x], t[y]) for x, y in pick], axis=1))
            return jnp.concatenate(blocks, axis=0)

        return read

    own_tab.wait()
    send_tab_k.wait_recv()
    k_tab = pltpu.make_async_copy(tab_k, k_s, loc.at[7])
    k_tab.start()
    send_i1.wait_recv()
    for i in range(4):
        weighted = fold_inverse(other, i, 4 + i)
        for m in range(2):
            orp[2 * i + m] = weighted[128 * m : 128 * m + 128, :]
    accb[0] = jnp.zeros((128, 128), BF16)
    for n in range(NT):
        link(accb, n, own_s[0, n], dot(t1_v[n], orp[cols1[0, n]]))
    read = coupling(accb, own_s, slice(0, 128))
    for i in range(4):
        spart[0, h, 64 * i : 64 * i + 64, :] = dot(xt[h * 4 + i, 0:64, :], read(i)).astype(BF16)

    send_t1.wait_recv()
    k_tab.wait()
    accc[0] = jnp.zeros((128, 256), BF16)
    for n in range(NT):
        link(accc, n, k_s[0, n], dot(t1_in[n], yk[k_s[4, n]]))
    read_e = coupling(accc, k_s, slice(128, 256))
    select_first(merged(accc, k_s, True), read_e, other)

    send_sr.wait_recv()
    sends_l = []
    for hs in range(2):
        own = dot(sr[0, hs], u1r[h])
        far = dot(spart[0, hs], u1r[other])
        lsr[hs] = (ksr[hs].astype(F32) - own - far).astype(BF16)
        sends_l.append(to_k(lsr.at[hs], lsr_in.at[hs], 5 + hs))
        sends_l[-1].start()

    for n in range(NT):
        before = own_s[2, n]
        link(acct, n, before, acct[n + 1].astype(F32))
        link(accv, n, before, accv[n + 1].astype(F32))
    for i in range(8):
        hs, i4 = i // 4, i % 4
        for q in range(2):
            e_at, o_at = own_s[3, 4 * i + 2 * q], own_s[3, 4 * i + 2 * q + 1]
            lanes = slice(128 * q, 128 * q + 128)
            swap = 64 * (i4 ^ 1)
            bss[64 * i : 64 * i + 64, lanes] = jnp.where(low64, acct[e_at], acct[o_at])
            bsr[64 * i : 64 * i + 64, lanes] = jnp.where(low64, acct[o_at], acct[e_at])
            vown[hs, swap : swap + 64, lanes] = jnp.where(low64, accv[e_at], accv[o_at])
    send_bsr = to_k(bsr, bsr_in, 7)
    send_bsr.start()

    send_tab_x.wait_recv()
    x_tab = pltpu.make_async_copy(tab_x, x_s, loc.at[8])
    x_tab.start()
    select_later(block_of(ams), block_of(ame), h)
    send_sr1 = to_k(sr.at[1, h], spart.at[1, h], 9)
    send_sr1.start()
    for i in range(4):
        spart[1, h, 64 * i : 64 * i + 64, :] = dot(xt[h * 4 + i, 192:256, :], read(i)).astype(BF16)

    sends_p = []
    for hs in range(2):
        sends_l[hs].wait_recv()
        for m in range(2):
            at = 256 * hs + 128 * m
            rows = slice(128 * m, 128 * m + 128)
            total = bss[at : at + 128, :].astype(F32) - dot(lsr[hs, rows, :], vown[h]) - dot(lsr_in[hs, rows, :], vown[other])
            p_out[at : at + 128, :] = total.astype(BF16)
            part = pl.ds(at, 128)
            sends_p.append(to_x(p_out.at[part], p_in.at[part], 4 + 2 * hs + m))
            sends_p[-1].start()

    select_later(merged(accc, k_s, False), read_e, other)
    for hs in range(2):
        own = dot(sr[0, hs], u1s[h])
        far = dot(spart[0, hs], u1s[other])
        lss[hs] = kss[0, hs].astype(F32) - own - far

    x_tab.wait()
    for send in sends_q:
        send.wait_recv()
    accxs[0] = jnp.zeros((64, 128), BF16)
    accxv[0] = jnp.zeros((64, 128), BF16)
    for n in range(NT):
        link(accxs, n, x_s[2, n], turned(srq_in[n % 8].astype(F32), x_s[5, n], n // 8))
        link(accxv, n, x_s[2, n], turned(vq_in[n % 8].astype(F32), x_s[5, n], 1 - n // 8))
    for i in range(8):
        hs, i4 = i // 4, i % 4
        for q in range(2):
            e_at, o_at = x_s[3, 4 * i + 2 * q], x_s[3, 4 * i + 2 * q + 1]
            lanes = slice(128 * q, 128 * q + 128)
            swap = 64 * (i4 ^ 1)
            vx[hs, swap : swap + 64, lanes] = jnp.where(low64, accxv[e_at], accxv[o_at])
            csr[64 * i : 64 * i + 64, lanes] = jnp.where(low64, accxs[o_at], accxs[e_at])
    send_csr = to_k(csr, csr_in, 8)
    send_csr.start()

    send_sr1.wait_recv()
    for hs in range(2):
        own = dot(sr[1, hs], u1s[h])
        far = dot(spart[1, hs], u1s[other])
        high, rest = halves(kss[1, hs].astype(F32) - own - far)
        for q in range(2):
            pack = packed(i2_v, hs, q)
            anti = jnp.concatenate([jnp.where(low64, 0.0, pack), jnp.where(low64, pack, 0.0)], axis=0)
            a_high, a_rest = halves(anti)
            rows = slice(128 * q, 128 * q + 128)
            total = dot(a_high, high[rows, :]) + dot(a_rest, high[rows, :]) + dot(a_high, rest[rows, :])
            uu[hs, rows, :] = total.astype(BF16)

    send_bsr.wait_recv()
    top = pl.multiple_of(c * 512, 512)
    bottom = pl.multiple_of(512 - c * 512, 512)
    for hs in range(2):
        rows = slice(256 * hs, 256 * hs + 256)
        total = lss[hs] - dot(lsr[hs], uu[h]) - dot(lsr_in[hs], uu[other])
        total = total - dot(bsr[rows, :], vx[h]) - dot(bsr_in[rows, :], vx[other])
        out_ref[0, pl.ds(top + 256 * hs, 256), :] = total.astype(BF16)
    send_csr.wait_recv()
    for hs in range(2):
        rows = slice(256 * hs, 256 * hs + 256)
        lss[hs] = dot(csr[rows, :], uu[h]) + dot(csr_in[rows, :], uu[other])
    for m in range(4):
        at = 128 * m
        rows = slice(128 * (m % 2), 128 * (m % 2) + 128)
        sends_p[m].wait_recv()
        total = p_in[at : at + 128, :].astype(F32) - lss[m // 2, rows, :]
        out_ref[0, pl.ds(bottom + at, 128), :] = total.astype(BF16)

    for send in (send_t1, send_i1, send_i2, send_tab_k, send_tab_x, send_sr, send_sr1, *sends_q, *sends_l, send_bsr, *sends_p, send_csr):
        send.wait_send()


def local(*args):
    schur, t1, rows1, cols1, count1, o1, i1, t2, rows2, cols2, count2, o2, i2 = args
    hbm = pl.BlockSpec(memory_space=pltpu.HBM)
    label = pltpu.SMEM((1, 16), jnp.int32)
    count = pltpu.SMEM((1,), jnp.int32)
    vmem = pltpu.VMEM
    table = vmem((8, 128), jnp.int32)
    table_s = pltpu.SMEM((8, 128), jnp.int32)
    tiles = vmem((16, 128, 128), BF16)
    panel = vmem((512, 256), BF16)
    panels = vmem((2, 256, 256), BF16)
    onehots = vmem((8, 128, 128), BF16)
    chained = vmem((17, 64, 128), BF16)
    quads = vmem((8, 64, 128), BF16)
    dma = pltpu.SemaphoreType.DMA
    scratch = [
        label, label, count, label, label, count,
        vmem((1024, 1024), BF16), tiles, tiles, tiles,
        vmem((8, 64, 64), F32), vmem((2, 4, 64, 64), F32), vmem((16, 128), jnp.int32), vmem((16, 128), jnp.int32),
        table, table, table, table_s, table_s, table_s,
        vmem((2, 4, 64, 128), BF16), vmem((8, 256, 256), BF16), vmem((8, 128, 256), BF16), onehots, onehots, vmem((8, 128, 64), BF16), vmem((4, 128, 128), BF16),
        vmem((17, 128, 128), BF16), vmem((17, 128, 256), BF16), chained, chained, chained, chained, vmem((16, 64, 128), BF16),
        quads, quads, quads, quads,
        vmem((1024, 256), BF16), vmem((1024, 256), BF16), vmem((1024, 512), BF16),
        panels, vmem((2, 2, 256, 256), BF16), vmem((2, 512, 256), BF16), vmem((2, 512, 256), BF16),
        vmem((2, 2, 256, 512), BF16), vmem((2, 2, 256, 512), BF16),
        vmem((2, 256, 256), F32), panels, panels, panels, panels, panels,
        panel, panel, panel, panel, panel, panel, panel,
        dma((16,)), dma((10,)), dma((10,)), dma((8,)), dma((8,)),
    ]
    large = [pltpu.with_memory_space_constraint(x, pltpu.HBM) for x in (schur, t1, t2, i1, i2, o1, o2)]
    return pl.pallas_call(
        kernel,
        out_shape=pltpu.VMEM((1, 1024, 256), BF16),
        in_specs=[hbm] * 13,
        out_specs=pl.BlockSpec(memory_space=pltpu.VMEM),
        scratch_shapes=scratch,
        compiler_params=pltpu.CompilerParams(collective_id=0, has_side_effects=True, vmem_limit_bytes=62 * 2**20),
    )(*large, rows1, cols1, count1, rows2, cols2, count2)


def solution(mesh):
    boxes = ("leaf", "blk")
    return jax.shard_map(
        local,
        mesh=mesh,
        in_specs=(
            P(boxes, None, None),
            P(boxes, None, None, None),
            P(boxes, None),
            P(boxes, None),
            P(boxes),
            P(),
            P(boxes, None, None, None),
            P(boxes, None, None, None),
            P(boxes, None),
            P(boxes, None),
            P(boxes),
            P(),
            P(boxes, None, None, None),
        ),
        out_specs=P(boxes, None, None),
        check_vma=False,
    )
```

```python
import jax
import jax.numpy as jnp
from jax import lax
from jax.experimental import pallas as pl
from jax.experimental.pallas import tpu as pltpu
from jax.sharding import PartitionSpec as P

MESH = pl.DeviceIdType.MESH
F32 = jnp.float32
BF16 = jnp.bfloat16
NT = 16


def dot(a, b):
    return jnp.dot(a, b, preferred_element_type=F32)


def chain_table(rows, cols, count, halved, lane):
    live = count[0]
    targets = [rows[0, n] * 4 + (cols[0, n] >> halved) for n in range(NT)]
    along = jnp.full((1, 128), -1, jnp.int32)
    columns = jnp.zeros((1, 128), jnp.int32)
    for n in range(NT):
        along = jnp.where(lane == n, targets[n], along)
        columns = jnp.where(lane == n, cols[0, n], columns)
    prev = jnp.zeros((1, 128), jnp.int32)
    last = jnp.zeros((1, 128), jnp.int32)
    for n in range(NT):
        value = jnp.where(n < live, n + 1, 0)
        prev = jnp.maximum(prev, jnp.where((along == targets[n]) & (lane > n), value, 0))
        last = jnp.maximum(last, jnp.where(lane == targets[n], value, 0))
    return prev, last, columns


def halves(value):
    high = value.astype(BF16)
    return high, (value - high.astype(F32)).astype(BF16)


def kernel(
    a_hbm, t1_hbm, t2_hbm, i1_hbm, i2_hbm, o1_hbm, o2_hbm,
    rows1_hbm, cols1_hbm, count1_hbm, rows2_hbm, cols2_hbm, count2_hbm,
    out_ref,
    rows1, cols1, count1, rows2, cols2, count2,
    a_v, t1_v, t1_in, t2_v, i1_v, i2_v, o1_v, o2_v,
    tab, tab_k, tab_x, own_s, k_s, x_s,
    pack1, xt, yk, orp, p2s, p2v, p2x,
    accb, accc, acct, accv, accxs, accxv, halfs, srq, srq_in, vq, vq_in,
    ams, amr, ame, ksr, kss, u1r, u1s, sr, spart,
    lss, lsr, lsr_in, uu, vown, vx,
    bss, bsr, bsr_in, csr, csr_in, p_out, p_in,
    loc, ksend, krecv, xsend, xrecv,
):
    leaf = lax.axis_index("leaf")
    c = lax.axis_index("blk")
    r = leaf // 2
    h = leaf - 2 * r
    other = 1 - h
    kid = {"leaf": leaf + 1 - 2 * h}
    xid = {"blk": 1 - c}

    def to_k(src, dst, n):
        return pltpu.make_async_remote_copy(
            src_ref=src, dst_ref=dst, send_sem=ksend.at[n], recv_sem=krecv.at[n],
            device_id=kid, device_id_type=MESH,
        )

    def to_x(src, dst, n):
        return pltpu.make_async_remote_copy(
            src_ref=src, dst_ref=dst, send_sem=xsend.at[n], recv_sem=xrecv.at[n],
            device_id=xid, device_id_type=MESH,
        )

    barrier = pltpu.get_barrier_semaphore()
    pl.semaphore_signal(barrier, inc=1, device_id=xid, device_id_type=MESH)
    pl.semaphore_signal(barrier, inc=1, device_id=kid, device_id_type=MESH)

    pairs = (
        (rows2_hbm, rows2), (cols2_hbm, cols2), (count2_hbm, count2),
        (rows1_hbm, rows1), (cols1_hbm, cols1), (count1_hbm, count1),
    )
    load_labels = [pltpu.make_async_copy(src, dst, loc.at[9 + n]) for n, (src, dst) in enumerate(pairs)]
    load_o1 = pltpu.make_async_copy(o1_hbm.at[2 * r + c], o1_v, loc.at[0])
    load_o2 = pltpu.make_async_copy(o2_hbm.at[r], o2_v, loc.at[1])
    load_t2 = pltpu.make_async_copy(t2_hbm.at[0], t2_v, loc.at[2])
    load_i2 = pltpu.make_async_copy(i2_hbm.at[0], i2_v.at[h], loc.at[3])
    load_i1 = pltpu.make_async_copy(i1_hbm.at[0], i1_v, loc.at[4])
    load_a = pltpu.make_async_copy(a_hbm.at[0], a_v, loc.at[5])
    load_t1 = pltpu.make_async_copy(t1_hbm.at[0], t1_v, loc.at[15])
    for load in (load_o2, *load_labels, load_t2, load_o1, load_i1, load_a, load_i2, load_t1):
        load.start()

    wide = lax.broadcasted_iota(jnp.int32, (128, 256), 1).astype(BF16)
    tall = lax.broadcasted_iota(jnp.int32, (256, 128), 0).astype(BF16)
    square = tall[0:128, :]
    low8 = lax.broadcasted_iota(jnp.int32, (8, 128), 1) < 64
    low64 = lax.broadcasted_iota(jnp.int32, (64, 128), 1) < 64
    low1024 = lax.broadcasted_iota(jnp.int32, (1024, 128), 1) < 64
    low128 = lax.broadcasted_iota(jnp.int32, (128, 128), 1) < 64
    lane = lax.broadcasted_iota(jnp.int32, (1, 128), 1)

    one, zero = jnp.asarray(1, BF16), jnp.asarray(0, BF16)

    def onehot(rows, index):
        return jnp.where(rows == index.astype(BF16), one, zero)

    load_o2.wait()
    base = pl.multiple_of(c * 8, 8)
    mine2 = o2_v[pl.ds(base, 8), :]
    theirs2 = o2_v[pl.ds(pl.multiple_of(8 - base, 8), 8), :]
    theirs2 = jnp.where(h == 0, theirs2, pltpu.roll(theirs2, 4, 0))
    columns2 = mine2.astype(F32).T
    for i in range(4):
        row = theirs2[i : i + 1, :]
        p2x[i] = onehot(square, pltpu.roll(row, 64, 1) if i % 2 else row)
    for k in range(8):
        p2s[k] = onehot(wide[:, 0:128], columns2[:, k : k + 1])

    def turned(value, column, wanted):
        return jnp.where((column & 1) == wanted, pltpu.roll(value, 64, 1), value)

    load_i1.wait()
    for i in range(4):
        pack1[h, i] = jnp.concatenate([i1_v[2 * i], i1_v[2 * i + 1]], axis=1).astype(BF16)
    for load in load_labels[:2]:
        load.wait()
    load_t2.wait()
    acct[0] = jnp.zeros((64, 128), BF16)
    accv[0] = jnp.zeros((64, 128), BF16)
    sends_q = []
    tops = []
    order = [n for m in range(8) for n in (m, m + 8)]
    for n in order:
        half = dot(t2_v[n], p2x[cols2[0, n]]).astype(BF16)
        both = dot(p2s[rows2[0, n]], half)
        top = both[0:64, :]
        halfs[n] = both[64:128, :].astype(BF16)
        acct[n + 1] = top.astype(BF16)
        tops.append(turned(top, cols2[0, n], n // 8))
        if n >= 8:
            srq[n - 8] = jnp.where(low64, tops[-2], tops[-1]).astype(BF16)

    pl.semaphore_wait(barrier, 2)
    load_i2.wait()
    load_t1.wait()
    send_t1 = to_k(t1_v, t1_in, 0)
    send_i1 = to_k(pack1.at[h], pack1.at[h], 1)
    send_i2 = to_k(i2_v.at[h], i2_v.at[h], 2)
    sends_q.append(to_x(srq, srq_in, 1))
    for send in (*sends_q, send_i2, send_i1, send_t1):
        send.start()

    for load in load_labels[2:]:
        load.wait()
    prev1, last1, cols_row1 = chain_table(rows1, cols1, count1, 1, lane)
    prev2, last2, cols_row2 = chain_table(rows2, cols2, count2, 0, lane)
    tab[0:1, :] = prev1
    tab[1:2, :] = last1
    tab[2:3, :] = prev2
    tab[3:4, :] = last2
    tab[4:5, :] = cols_row1
    tab[5:6, :] = cols_row2
    tab[6:8, :] = jnp.zeros((2, 128), jnp.int32)
    own_tab = pltpu.make_async_copy(tab, own_s, loc.at[6])
    own_tab.start()
    send_tab_k = to_k(tab, tab_k, 3)
    send_tab_k.start()
    send_tab_x = to_x(tab, tab_x, 0)
    send_tab_x.start()

    load_o1.wait()
    even = o1_v[pl.ds(0, 8, stride=2), :]
    odd = o1_v[pl.ds(1, 8, stride=2), :]
    shift = jnp.where(low8, 0, 128)
    skel = jnp.where(low8, even, pltpu.roll(odd, 64, 1)) + shift
    redu = jnp.where(low8, pltpu.roll(even, 64, 1), odd) + shift
    comp = jnp.take_along_axis(skel, mine2, axis=1, mode="promise_in_bounds")
    columns = jnp.concatenate([comp, redu], axis=0).astype(F32).T
    comp_own = jnp.where(h == 0, comp, pltpu.roll(comp, 4, 0))
    redu_own = jnp.where(h == 0, redu, pltpu.roll(redu, 4, 0))
    for k in range(8):
        xt[k, 0:64, :] = onehot(wide[0:64, :], columns[0:64, k : k + 1])
        xt[k, 64:128, 0:128] = onehot(wide[0:64, 0:128], columns[0:64, 8 + k : 9 + k])
        xt[k, 64:128, 128:256] = jnp.zeros((64, 128), BF16)
        xt[k, 128:192, 0:128] = jnp.zeros((64, 128), BF16)
        xt[k, 128:192, 128:256] = onehot(wide[0:64, 128:256], columns[64:128, 8 + k : 9 + k])

    def packed(ref, hs, q):
        return jnp.concatenate([ref[hs, 2 * q], ref[hs, 2 * q + 1]], axis=1)

    def fold_inverse(hs, i, index):
        pack = pack1[hs, i]
        diag = jnp.concatenate([jnp.where(low64, pack, zero), jnp.where(low64, zero, pack)], axis=0)
        return dot(onehot(tall, redu_own[index : index + 1, :]), diag).astype(BF16)

    for i in range(4):
        row = comp_own[i : i + 1, :]
        skeleton = onehot(tall, pltpu.roll(row, 64, 1) if i % 2 else row)
        weighted = fold_inverse(h, i, i)
        for m in range(2):
            yk[2 * i + m, :, 0:128] = skeleton[128 * m : 128 * m + 128, :]
            yk[2 * i + m, :, 128:256] = weighted[128 * m : 128 * m + 128, :]

    def select_first(read_r, read_e, hs):
        for i in range(4):
            block = dot(xt[hs * 4 + i, 0:192, :], read_r(i)).astype(BF16)
            rows = slice(64 * i, 64 * i + 64)
            ksr[hs, rows, :] = block[0:64, :]
            u1r[hs, 128 * i : 128 * i + 128, :] = block[64:192, :]
            sr[0, hs, rows, :] = dot(xt[hs * 4 + i, 0:64, :], read_e(i)).astype(BF16)

    def select_later(read_s, read_e, hs):
        for i in range(4):
            block = dot(xt[hs * 4 + i], read_s(i)).astype(BF16)
            rows = slice(64 * i, 64 * i + 64)
            kss[0, hs, rows, :] = block[0:64, :]
            u1s[hs, 128 * i : 128 * i + 128, :] = block[64:192, :]
            kss[1, hs, rows, :] = block[192:256, :]
            sr[1, hs, rows, :] = dot(xt[hs * 4 + i, 192:256, :], read_e(i)).astype(BF16)

    load_a.wait()
    for q in range(2):
        part = []
        for i in (2 * q, 2 * q + 1):
            weights = yk[2 * i : 2 * i + 2].reshape(256, 256)
            both = dot(a_v[:, 256 * i : 256 * i + 256], weights)
            part.append(both[:, 0:128])
            ame[:, 128 * i : 128 * i + 128] = both[:, 128:256].astype(BF16)
        ams[:, 128 * q : 128 * q + 128] = jnp.where(low1024, part[0], part[1]).astype(BF16)
        amr[:, 128 * q : 128 * q + 128] = jnp.where(low1024, part[1], part[0]).astype(BF16)

    def block_of(ref):
        return lambda i: ref[256 * i : 256 * i + 256, :]

    select_first(block_of(amr), block_of(ame), h)
    send_sr = to_k(sr.at[0, h], spart.at[0, h], 4)
    send_sr.start()

    send_i2.wait_recv()
    for k in range(8):
        p2v[k] = jnp.concatenate(halves(i2_v[k // 4, k % 4]), axis=0)
    bottoms = []
    for n in order:
        both = dot(p2v[rows2[0, n]], halfs[n])
        bottom = both[0:64, :] + both[64:128, :]
        accv[n + 1] = bottom.astype(BF16)
        bottoms.append(turned(bottom, cols2[0, n], 1 - n // 8))
        if n >= 8:
            vq[n - 8] = jnp.where(low64, bottoms[-2], bottoms[-1]).astype(BF16)
        if n in (11, 15):
            part = pl.ds(n - 11, 4)
            sends_q.append(to_x(vq.at[part], vq_in.at[part], 2 + (n - 11) // 4))
            sends_q[-1].start()

    def link(acc, n, before, value):
        acc[n + 1] = (value + acc[before].astype(F32)).astype(BF16)

    def coupling(acc, table, lanes):
        def read(i):
            blocks = [[acc[table[1, 4 * j + m], :, lanes] for m in range(4)] for j in (2 * i, 2 * i + 1)]
            return jnp.concatenate([jnp.concatenate(row, axis=1) for row in blocks], axis=0)

        return read

    def merged(acc, table, swapped):
        def read(i):
            blocks = []
            for j in (2 * i, 2 * i + 1):
                t = [acc[table[1, 4 * j + m], :, 0:128] for m in range(4)]
                pick = ((1, 0), (3, 2)) if swapped else ((0, 1), (2, 3))
                blocks.append(jnp.concatenate([jnp.where(low128, t[x], t[y]) for x, y in pick], axis=1))
            return jnp.concatenate(blocks, axis=0)

        return read

    own_tab.wait()
    send_tab_k.wait_recv()
    k_tab = pltpu.make_async_copy(tab_k, k_s, loc.at[7])
    k_tab.start()
    send_i1.wait_recv()
    for i in range(4):
        weighted = fold_inverse(other, i, 4 + i)
        for m in range(2):
            orp[2 * i + m] = weighted[128 * m : 128 * m + 128, :]
    accb[0] = jnp.zeros((128, 128), BF16)
    for n in range(NT):
        link(accb, n, own_s[0, n], dot(t1_v[n], orp[cols1[0, n]]))
    read = coupling(accb, own_s, slice(0, 128))
    for i in range(4):
        spart[0, h, 64 * i : 64 * i + 64, :] = dot(xt[h * 4 + i, 0:64, :], read(i)).astype(BF16)

    send_t1.wait_recv()
    k_tab.wait()
    accc[0] = jnp.zeros((128, 256), BF16)
    for n in range(NT):
        link(accc, n, k_s[0, n], dot(t1_in[n], yk[k_s[4, n]]))
    read_e = coupling(accc, k_s, slice(128, 256))
    select_first(merged(accc, k_s, True), read_e, other)

    send_sr.wait_recv()
    sends_l = []
    for hs in range(2):
        own = dot(sr[0, hs], u1r[h])
        far = dot(spart[0, hs], u1r[other])
        lsr[hs] = (ksr[hs].astype(F32) - own - far).astype(BF16)
        sends_l.append(to_k(lsr.at[hs], lsr_in.at[hs], 5 + hs))
        sends_l[-1].start()

    for k in range(8):
        xt[k, 192:256, :] = onehot(wide[64:128, :], columns[64:128, k : k + 1])

    for n in range(NT):
        before = own_s[2, n]
        link(acct, n, before, acct[n + 1].astype(F32))
        link(accv, n, before, accv[n + 1].astype(F32))
    for i in range(8):
        hs, i4 = i // 4, i % 4
        for q in range(2):
            e_at, o_at = own_s[3, 4 * i + 2 * q], own_s[3, 4 * i + 2 * q + 1]
            lanes = slice(128 * q, 128 * q + 128)
            swap = 64 * (i4 ^ 1)
            bss[64 * i : 64 * i + 64, lanes] = jnp.where(low64, acct[e_at], acct[o_at])
            bsr[64 * i : 64 * i + 64, lanes] = jnp.where(low64, acct[o_at], acct[e_at])
            vown[hs, swap : swap + 64, lanes] = jnp.where(low64, accv[e_at], accv[o_at])
    send_bsr = to_k(bsr, bsr_in, 7)
    send_bsr.start()

    send_tab_x.wait_recv()
    x_tab = pltpu.make_async_copy(tab_x, x_s, loc.at[8])
    x_tab.start()
    select_later(block_of(ams), block_of(ame), h)
    send_sr1 = to_k(sr.at[1, h], spart.at[1, h], 9)
    send_sr1.start()
    for i in range(4):
        spart[1, h, 64 * i : 64 * i + 64, :] = dot(xt[h * 4 + i, 192:256, :], read(i)).astype(BF16)

    sends_p = []
    for hs in range(2):
        sends_l[hs].wait_recv()
        for m in range(2):
            at = 256 * hs + 128 * m
            rows = slice(128 * m, 128 * m + 128)
            total = bss[at : at + 128, :].astype(F32) - dot(lsr[hs, rows, :], vown[h]) - dot(lsr_in[hs, rows, :], vown[other])
            p_out[at : at + 128, :] = total.astype(BF16)
            part = pl.ds(at, 128)
            sends_p.append(to_x(p_out.at[part], p_in.at[part], 4 + 2 * hs + m))
            sends_p[-1].start()

    select_later(merged(accc, k_s, False), read_e, other)
    for hs in range(2):
        own = dot(sr[0, hs], u1s[h])
        far = dot(spart[0, hs], u1s[other])
        lss[hs] = kss[0, hs].astype(F32) - own - far

    x_tab.wait()
    for send in sends_q:
        send.wait_recv()
    accxs[0] = jnp.zeros((64, 128), BF16)
    accxv[0] = jnp.zeros((64, 128), BF16)
    for n in range(NT):
        link(accxs, n, x_s[2, n], turned(srq_in[n % 8].astype(F32), x_s[5, n], n // 8))
        link(accxv, n, x_s[2, n], turned(vq_in[n % 8].astype(F32), x_s[5, n], 1 - n // 8))
    for i in range(8):
        hs, i4 = i // 4, i % 4
        for q in range(2):
            e_at, o_at = x_s[3, 4 * i + 2 * q], x_s[3, 4 * i + 2 * q + 1]
            lanes = slice(128 * q, 128 * q + 128)
            swap = 64 * (i4 ^ 1)
            vx[hs, swap : swap + 64, lanes] = jnp.where(low64, accxv[e_at], accxv[o_at])
            csr[64 * i : 64 * i + 64, lanes] = jnp.where(low64, accxs[o_at], accxs[e_at])
    send_csr = to_k(csr, csr_in, 8)
    send_csr.start()

    send_sr1.wait_recv()
    for hs in range(2):
        own = dot(sr[1, hs], u1s[h])
        far = dot(spart[1, hs], u1s[other])
        high, rest = halves(kss[1, hs].astype(F32) - own - far)
        for q in range(2):
            pack = packed(i2_v, hs, q)
            anti = jnp.concatenate([jnp.where(low64, 0.0, pack), jnp.where(low64, pack, 0.0)], axis=0)
            a_high, a_rest = halves(anti)
            rows = slice(128 * q, 128 * q + 128)
            total = dot(a_high, high[rows, :]) + dot(a_rest, high[rows, :]) + dot(a_high, rest[rows, :])
            uu[hs, rows, :] = total.astype(BF16)

    send_bsr.wait_recv()
    top = pl.multiple_of(c * 512, 512)
    bottom = pl.multiple_of(512 - c * 512, 512)
    for hs in range(2):
        rows = slice(256 * hs, 256 * hs + 256)
        total = lss[hs] - dot(lsr[hs], uu[h]) - dot(lsr_in[hs], uu[other])
        total = total - dot(bsr[rows, :], vx[h]) - dot(bsr_in[rows, :], vx[other])
        out_ref[0, pl.ds(top + 256 * hs, 256), :] = total.astype(BF16)
    send_csr.wait_recv()
    for hs in range(2):
        rows = slice(256 * hs, 256 * hs + 256)
        lss[hs] = dot(csr[rows, :], uu[h]) + dot(csr_in[rows, :], uu[other])
    for m in range(4):
        at = 128 * m
        rows = slice(128 * (m % 2), 128 * (m % 2) + 128)
        sends_p[m].wait_recv()
        total = p_in[at : at + 128, :].astype(F32) - lss[m // 2, rows, :]
        out_ref[0, pl.ds(bottom + at, 128), :] = total.astype(BF16)

    for send in (send_t1, send_i1, send_i2, send_tab_k, send_tab_x, send_sr, send_sr1, *sends_q, *sends_l, send_bsr, *sends_p, send_csr):
        send.wait_send()


def local(*args):
    schur, t1, rows1, cols1, count1, o1, i1, t2, rows2, cols2, count2, o2, i2 = args
    hbm = pl.BlockSpec(memory_space=pltpu.HBM)
    label = pltpu.SMEM((1, 16), jnp.int32)
    count = pltpu.SMEM((1,), jnp.int32)
    vmem = pltpu.VMEM
    table = vmem((8, 128), jnp.int32)
    table_s = pltpu.SMEM((8, 128), jnp.int32)
    tiles = vmem((16, 128, 128), BF16)
    panel = vmem((512, 256), BF16)
    panels = vmem((2, 256, 256), BF16)
    onehots = vmem((8, 128, 128), BF16)
    chained = vmem((17, 64, 128), BF16)
    quads = vmem((8, 64, 128), BF16)
    dma = pltpu.SemaphoreType.DMA
    scratch = [
        label, label, count, label, label, count,
        vmem((1024, 1024), BF16), tiles, tiles, tiles,
        vmem((8, 64, 64), F32), vmem((2, 4, 64, 64), F32), vmem((16, 128), jnp.int32), vmem((16, 128), jnp.int32),
        table, table, table, table_s, table_s, table_s,
        vmem((2, 4, 64, 128), BF16), vmem((8, 256, 256), BF16), vmem((8, 128, 256), BF16), onehots, onehots, vmem((8, 128, 64), BF16), vmem((4, 128, 128), BF16),
        vmem((17, 128, 128), BF16), vmem((17, 128, 256), BF16), chained, chained, chained, chained, vmem((16, 64, 128), BF16),
        quads, quads, quads, quads,
        vmem((1024, 256), BF16), vmem((1024, 256), BF16), vmem((1024, 512), BF16),
        panels, vmem((2, 2, 256, 256), BF16), vmem((2, 512, 256), BF16), vmem((2, 512, 256), BF16),
        vmem((2, 2, 256, 512), BF16), vmem((2, 2, 256, 512), BF16),
        vmem((2, 256, 256), F32), panels, panels, panels, panels, panels,
        panel, panel, panel, panel, panel, panel, panel,
        dma((16,)), dma((10,)), dma((10,)), dma((8,)), dma((8,)),
    ]
    large = [pltpu.with_memory_space_constraint(x, pltpu.HBM) for x in (schur, t1, t2, i1, i2, o1, o2)]
    return pl.pallas_call(
        kernel,
        out_shape=pltpu.VMEM((1, 1024, 256), BF16),
        in_specs=[hbm] * 13,
        out_specs=pl.BlockSpec(memory_space=pltpu.VMEM),
        scratch_shapes=scratch,
        compiler_params=pltpu.CompilerParams(collective_id=0, has_side_effects=True, vmem_limit_bytes=62 * 2**20),
    )(*large, rows1, cols1, count1, rows2, cols2, count2)


def solution(mesh):
    boxes = ("leaf", "blk")
    return jax.shard_map(
        local,
        mesh=mesh,
        in_specs=(
            P(boxes, None, None),
            P(boxes, None, None, None),
            P(boxes, None),
            P(boxes, None),
            P(boxes),
            P(),
            P(boxes, None, None, None),
            P(boxes, None, None, None),
            P(boxes, None),
            P(boxes, None),
            P(boxes),
            P(),
            P(boxes, None, None, None),
        ),
        out_specs=P(boxes, None, None),
        check_vma=False,
    )
```
